256 devices in a mesh: seq: 64 (over x_hi, z, y), tp: 4 (over x_lo, core).
Axes of the slice: x: 4 (x_hi: 2, x_lo: 2; x = x_hi * 2 + x_lo), y: 4, z: 8, core: 2. Of those that a mesh axis runs over, the one named last changes fastest.
Arguments:
- query_rows: bfloat16 [16384, 4096], P('seq', 'tp'), may hold values from -130 to 130
- key_rows: bfloat16 [16384, 4096], P('seq', 'tp'), may hold values from -8 to 8
- value_rows: bfloat16 [16384, 4096], P('seq', 'tp'), may hold values from -6 to 6
- cotangent: bfloat16 [16384, 4096], P('seq', 'tp'), may hold values from -6 to 6
- global_pos: int32 [256], P('seq'), may hold values from 0 to 16383, as said below
- partner_mask: int32 [1], replicated, may hold values from 1 to 63
- rand_block: int32 [1, 64], replicated, may hold values from 0 to 1
Outputs:
- attention: bfloat16 [16384, 4096], P('seq', 'tp')
- grad_queries: bfloat16 [16384, 4096], P('seq', 'tp')
- grad_keys: bfloat16 [16384, 4096], P('seq', 'tp')
- grad_values: bfloat16 [16384, 4096], P('seq', 'tp')
The draws below stay inside these ranges and needn't reach their ends.
Inputs may be any that keep to these rules, and one draw needn't show every extreme that they name: `global_pos`: the tokens of run d (positions d * 256 onward) hold exactly 4 global positions; all are distinct and in increasing order.
All inputs are finite; a program needn't handle non-finite values.
Results may differ from the reference program's by a relative error of at most 0.011.
Values may be sent and summed in bfloat16 or wider, within the bound.
A program may use at most 128 MiB of HBM per device.

```python
import jax
import jax.numpy as jnp
from jax import lax

HEADS = 32
HEAD_DIM = 128
BLK = 128
BLK_DEV = 2
ROUNDS = 1
GLOB_DEV = 4
D = 4096
TOK_DEV = 256
SEQ_LEN = 16384
GLOBALS = 256
SHARDS = 64
N_SEQ = 64


def global_rows_draw(key):
    shard_count = GLOBALS // GLOB_DEV
    split_keys = jax.random.split(jax.random.fold_in(key, 7), shard_count)

    def pick_rows(one_key):
        return jnp.sort(jax.random.permutation(one_key, TOK_DEV)[:GLOB_DEV])
    picks = jax.vmap(pick_rows)(split_keys)
    return (picks + jnp.arange(shard_count, dtype=jnp.int32)[:, None] * TOK_DEV).reshape(-1).astype(jnp.int32)


def key_draw(key):
    base = jnp.clip(jax.random.normal(jax.random.fold_in(key, 12), (SEQ_LEN, D), jnp.float32), -6.0, 6.0)
    return base


def draw_global_pos(key, part):
    return global_rows_draw(key)


def draw_key_rows(key, part):
    return key_draw(key).astype(jnp.bfloat16)


def draw_query_rows(key, part):
    base = jnp.clip(jax.random.normal(jax.random.fold_in(key, 11), (SEQ_LEN, D), jnp.float32), -6.0, 6.0)
    return base.astype(jnp.bfloat16)


def set_ends(entries, key, low, top_value):
    index_at = [jax.random.randint(jax.random.fold_in(key, axis), (), 0, length) for axis, length in enumerate(entries.shape)]
    longest = entries.shape.index(max(entries.shape))
    neighbour = index_at[:longest] + [(index_at[longest] + 1) % entries.shape[longest]] + index_at[longest + 1:]
    return entries.at[tuple(index_at)].set(low).at[tuple(neighbour)].set(top_value)


def block_levels(stream_key, dims, shards, least, high):
    def one(axis_at, shards_of):
        heights = jax.random.uniform(jax.random.fold_in(jax.random.fold_in(stream_key, 6), axis_at), (shards_of,), jnp.float32, least / len(shards), high / len(shards))
        return jnp.repeat(jnp.exp(heights), dims[axis_at] // shards_of).reshape((-1,) + (1,) * (len(dims) - axis_at - 1))

    gain = one(*shards[0])
    for cut in shards[1:]:
        gain = gain * one(*cut)
    return gain


def gaussian(key, shape, scale, bound, pieces=(), held_as=jnp.bfloat16):
    loudness = block_levels(key, shape, pieces, -0.22, 0.18) if pieces else 1.0
    drawn = jax.random.normal(key, shape, jnp.float32) * scale * loudness
    return jnp.minimum(jnp.maximum(drawn, -bound), bound).astype(held_as)


def setup_inputs(seed: int = 0) -> dict:
    arg_keys = jax.random.split(jax.random.key(seed), 8)
    return {
        "query_rows": draw_query_rows(jax.random.fold_in(arg_keys[7], 71), 0),
        "key_rows": draw_key_rows(jax.random.fold_in(arg_keys[7], 71), 0),
        "value_rows": gaussian(arg_keys[2], (SEQ_LEN, D), 1.0, 6.0, ((0, 64), (1, 4))),
        "cotangent": gaussian(arg_keys[3], (SEQ_LEN, D), 1.0, 6.0, ((0, 64), (1, 4))),
        "global_pos": draw_global_pos(jax.random.fold_in(arg_keys[7], 71), 0),
        "partner_mask": jax.random.randint(arg_keys[5], (ROUNDS,), 1, N_SEQ).astype(jnp.int32),
        "rand_block": set_ends(jax.random.randint(arg_keys[6], (ROUNDS, SHARDS), 0, BLK_DEV), jax.random.fold_in(arg_keys[6], 1), 0, BLK_DEV - 1).astype(jnp.int32),
    }


def attend(query_inputs, gathered_keys, gathered_values, usable, incoming_gradient):
    softmax_scale_factor = query_inputs.shape[-1] ** -0.5
    logit_scores = jnp.einsum("crj,prj->rcp", query_inputs.astype(jnp.float32), gathered_keys.astype(jnp.float32)) * softmax_scale_factor
    logit_scores = jnp.where(usable[None, None, :], logit_scores, -1e30)
    maxima = jnp.max(logit_scores, axis=2, keepdims=True)
    raised = jnp.exp(logit_scores - maxima)
    totals = jnp.sum(raised, axis=2, keepdims=True)
    chances = raised / totals
    attention_weight_rows = chances.astype(jnp.bfloat16)
    attention_output = jnp.einsum("bxl,lby->xby", attention_weight_rows.astype(jnp.float32), gathered_values.astype(jnp.float32)).astype(jnp.bfloat16)
    incoming_gradient_float = incoming_gradient.astype(jnp.float32)
    deltas = jnp.transpose(jnp.sum(incoming_gradient_float * attention_output.astype(jnp.float32), axis=2))[:, :, None]
    probability_gradient = jnp.einsum("crj,prj->rcp", incoming_gradient_float, gathered_values.astype(jnp.float32))
    scaled_scores = (chances * (probability_gradient - deltas) * softmax_scale_factor).astype(jnp.bfloat16)
    query_gradient_rows = jnp.einsum("bxl,lby->xby", scaled_scores.astype(jnp.float32), gathered_keys.astype(jnp.float32))
    key_gradient_rows = jnp.einsum("cgi,gcx->icx", scaled_scores.astype(jnp.float32), query_inputs.astype(jnp.float32))
    value_gradient_rows = jnp.einsum("cgi,gcx->icx", attention_weight_rows.astype(jnp.float32), incoming_gradient_float)
    return attention_output, query_gradient_rows, key_gradient_rows, value_gradient_rows


def reference(query_rows, key_rows, value_rows, cotangent, global_pos, partner_mask, rand_block):
    seq_total = query_rows.shape[0]
    query_per_head = query_rows.reshape(seq_total, HEADS, HEAD_DIM)
    key_per_head = key_rows.reshape(seq_total, HEADS, HEAD_DIM)
    value_per_head = value_rows.reshape(seq_total, HEADS, HEAD_DIM)
    cotangent_head_rows = cotangent.reshape(seq_total, HEADS, HEAD_DIM)
    block_count = seq_total // BLK
    global_marks = jnp.zeros((seq_total,), jnp.float32).at[global_pos].set(1.0)
    sparse_cot = jnp.where(global_marks[:, None, None] > 0.5, jnp.zeros_like(cotangent_head_rows), cotangent_head_rows)
    global_keys = key_per_head[global_pos]
    global_values = value_per_head[global_pos]
    padding = jnp.zeros((BLK, HEADS, HEAD_DIM), jnp.bfloat16)
    padded_keys = jnp.concatenate([padding, key_per_head, padding], axis=0)
    padded_values = jnp.concatenate([padding, value_per_head, padding], axis=0)
    shared_count = ROUNDS * BLK + GLOBALS
    grad_init = jnp.zeros((seq_total + 2 * BLK, HEADS, HEAD_DIM), jnp.float32)

    def block_step(carried, number):
        grad_keys, grad_values = carried
        begin = number * BLK
        device = number // BLK_DEV
        key_parts = [lax.dynamic_slice_in_dim(padded_keys, begin, 3 * BLK, 0)]
        value_parts = [lax.dynamic_slice_in_dim(padded_values, begin, 3 * BLK, 0)]
        offsets = []
        for turn_index in range(ROUNDS):
            partner = jnp.bitwise_xor(device, partner_mask[turn_index])
            first_row = ((partner * BLK_DEV + rand_block[turn_index, device]) * BLK).astype(jnp.int32)
            offsets.append(first_row)
            key_parts.append(lax.dynamic_slice_in_dim(key_per_head, first_row, BLK, 0))
            value_parts.append(lax.dynamic_slice_in_dim(value_per_head, first_row, BLK, 0))
        key_parts.append(global_keys)
        value_parts.append(global_values)
        usable = jnp.concatenate([jnp.full((BLK,), number > 0), jnp.ones((BLK,), bool), jnp.full((BLK,), number < block_count - 1), jnp.ones((shared_count,), bool)])
        attention_output, query_gradient_rows, key_gradient_rows, value_gradient_rows = attend(
            lax.dynamic_slice_in_dim(query_per_head, begin, BLK, 0),
            jnp.concatenate(key_parts, axis=0),
            jnp.concatenate(value_parts, axis=0),
            usable,
            lax.dynamic_slice_in_dim(sparse_cot, begin, BLK, 0))
        grad_keys = lax.dynamic_update_slice_in_dim(grad_keys, lax.dynamic_slice_in_dim(grad_keys, begin, 3 * BLK, 0) + key_gradient_rows[:3 * BLK], begin, 0)
        grad_values = lax.dynamic_update_slice_in_dim(grad_values, lax.dynamic_slice_in_dim(grad_values, begin, 3 * BLK, 0) + value_gradient_rows[:3 * BLK], begin, 0)
        for turn_index in range(ROUNDS):
            landing = offsets[turn_index] + BLK
            lower = 3 * BLK + turn_index * BLK
            grad_keys = lax.dynamic_update_slice_in_dim(grad_keys, lax.dynamic_slice_in_dim(grad_keys, landing, BLK, 0) + key_gradient_rows[lower:lower + BLK], landing, 0)
            grad_values = lax.dynamic_update_slice_in_dim(grad_values, lax.dynamic_slice_in_dim(grad_values, landing, BLK, 0) + value_gradient_rows[lower:lower + BLK], landing, 0)
        tail_start = 3 * BLK + ROUNDS * BLK
        grad_keys = grad_keys.at[global_pos + BLK].add(key_gradient_rows[tail_start:])
        grad_values = grad_values.at[global_pos + BLK].add(value_gradient_rows[tail_start:])
        return (grad_keys, grad_values), (attention_output, query_gradient_rows)

    (grad_keys, grad_values), (sparse_out, sparse_dq) = lax.scan(block_step, (grad_init, grad_init), jnp.arange(block_count, dtype=jnp.int32))

    def per_head(inputs):
        query_one, key_one, value_one, cot_one = inputs
        result = attend(query_one[:, None, :], key_one[:, None, :], value_one[:, None, :], jnp.ones((seq_total,), bool), cot_one[:, None, :])
        return tuple(member[:, 0, :] for member in result)

    heads_first = (1, 0, 2)
    global_out, global_dq, global_dk, global_dv = lax.map(per_head, (
        jnp.transpose(query_per_head[global_pos], heads_first),
        jnp.transpose(key_per_head, heads_first),
        jnp.transpose(value_per_head, heads_first),
        jnp.transpose(cotangent_head_rows[global_pos], heads_first)))
    attention = sparse_out.reshape(seq_total, HEADS, HEAD_DIM).at[global_pos].set(jnp.transpose(global_out, heads_first))
    grad_q = sparse_dq.reshape(seq_total, HEADS, HEAD_DIM).at[global_pos].add(jnp.transpose(global_dq, heads_first))
    grad_k = grad_keys[BLK:BLK + seq_total] + jnp.transpose(global_dk, heads_first)
    grad_v = grad_values[BLK:BLK + seq_total] + jnp.transpose(global_dv, heads_first)
    width_all = HEADS * HEAD_DIM
    return (attention.reshape(seq_total, width_all),
            grad_q.reshape(seq_total, width_all).astype(jnp.bfloat16),
            grad_k.reshape(seq_total, width_all).astype(jnp.bfloat16),
            grad_v.reshape(seq_total, width_all).astype(jnp.bfloat16))
```

```python
import functools

import jax
import jax.numpy as jnp
from jax import lax
from jax.experimental import pallas as pl
from jax.experimental.pallas import tpu as pltpu
from jax.sharding import PartitionSpec as P

HEAD_DIM = 128
BLK = 128
NX, NZ, NY = 2, 8, 4
NP = NX * NY
SCALE = HEAD_DIM**-0.5
MESH = pl.DeviceIdType.MESH
F32 = jnp.float32
BF16 = jnp.bfloat16


def nt(a, b):
    return lax.dot_general(a, b, (((1,), (1,)), ((), ())), preferred_element_type=F32)


def nn(a, b):
    return lax.dot_general(a, b, (((1,), (0,)), ((), ())), preferred_element_type=F32)


def tn(a, b):
    return lax.dot_general(a, b, (((0,), (0,)), ((), ())), preferred_element_type=F32)


def place():
    me = lax.axis_index("seq")
    return me, me // (NZ * NY), (me // NY) % NZ, me % NY


def seq_of(x, z, y):
    return (x * NZ + z) * NY + y


def greet(peers):
    barrier = pltpu.get_barrier_semaphore()
    for peer in peers:
        pl.semaphore_signal(barrier, inc=1, device_id=peer, device_id_type=MESH)
    pl.semaphore_wait(barrier, len(peers))


def plane_peers(x, z, y, tp):
    peers = []
    for offset in range(1, NP):
        dx, dy = offset // NY, offset % NY
        px, py = lax.rem(x + dx, NX), lax.rem(y + dy, NY)
        peers.append((offset, px * NY + py, (seq_of(px, z, py), tp)))
    return peers


def ring_peers(x, z, y, tp):
    return (seq_of(x, lax.rem(z + 1, NZ), y), tp), (seq_of(x, lax.rem(z + NZ - 1, NZ), y), tp)


def line_peers(me, tp):
    return (lax.rem(me + 1, NX * NZ * NY), tp), (lax.rem(me + NX * NZ * NY - 1, NX * NZ * NY), tp)


def remote(src, dst, send, recv, device):
    return pltpu.make_async_remote_copy(
        src_ref=src, dst_ref=dst, send_sem=send, recv_sem=recv, device_id=device, device_id_type=MESH
    )


def steps_of(array):
    return (4, 3) if array < 2 else (3, 4)


def gather_kernel(
    q_ref, k_ref, v_ref, c_ref, pos_ref, gath_ref, prev_ref, next_ref,
    piece_ref, plane_send, plane_recv, ring_send, ring_recv, edge_send, edge_recv,
):
    me, x, z, y = place()
    tp = lax.axis_index("tp")
    peers = plane_peers(x, z, y, tp)
    right, left = ring_peers(x, z, y, tp)
    after, before = line_peers(me, tp)
    mine = x * NY + y

    rows = lax.broadcasted_iota(jnp.int32, (16, 256), 0)
    columns = lax.broadcasted_iota(jnp.int32, (16, 256), 1)
    hit = columns == pos_ref[...]
    total = jnp.zeros((16, q_ref.shape[1]), F32)
    for number, ref in enumerate((q_ref, k_ref, v_ref, c_ref)):
        pick = jnp.where(hit & (rows // 4 == number), 1.0, 0.0).astype(BF16)
        total = total + nn(pick, ref[...])
    piece_ref[mine] = total.astype(BF16)

    greet([peer for _, _, peer in peers] + [right, left, after, before])
    copies = []
    for offset, _, peer in peers:
        copy = remote(
            piece_ref.at[mine], piece_ref.at[mine], plane_send.at[offset], plane_recv.at[offset], peer
        )
        copy.start()
        copies.append(copy)
    edges = []
    for number, ref in enumerate((k_ref, v_ref)):
        edges.append(
            remote(ref.at[pl.ds(BLK, BLK)], prev_ref.at[number], edge_send.at[number], edge_recv.at[number], after)
        )
        edges.append(
            remote(ref.at[pl.ds(0, BLK)], next_ref.at[number], edge_send.at[2 + number], edge_recv.at[2 + number], before)
        )
    for copy in copies:
        copy.wait()

    out_row = lax.broadcasted_iota(jnp.int32, (32, 128), 0)
    in_row = lax.broadcasted_iota(jnp.int32, (32, 128), 1)
    pieces = piece_ref[...].reshape(128, -1)
    for number in range(4):
        pick = jnp.where(in_row == (out_row // 4) * 16 + number * 4 + out_row % 4, 1.0, 0.0)
        gath_ref[z, number] = nn(pick.astype(BF16), pieces).astype(BF16)

    def hop(way, step, number):
        shift = lax.rem(z + NZ - step + 1, NZ) if way == 0 else lax.rem(z + step - 1, NZ)
        slot = (way * 4 + step - 1) * 4 + number
        part = gath_ref.at[shift, number]
        return remote(part, part, ring_send.at[slot], ring_recv.at[slot], right if way == 0 else left)

    flying = {}
    for number in range(4):
        for way in range(2):
            flying[way, 1, number] = hop(way, 1, number)
            flying[way, 1, number].start()
    for edge in edges:
        edge.start()
    for step in range(1, 5):
        for number in range(4):
            for way in range(2):
                if step <= steps_of(number)[way]:
                    flying[way, step, number].wait_recv()
                    if step < steps_of(number)[way]:
                        flying[way, step + 1, number] = hop(way, step + 1, number)
                        flying[way, step + 1, number].start()
    for copy in flying.values():
        copy.wait_send()
    for edge in edges:
        edge.wait()


def attend_kernel(
    q_ref, k_ref, v_ref, c_ref, keep_ref, bias_ref, prev_ref, next_ref, rand_ref, gath_ref,
    out_ref, dq_ref, dk_ref, dv_ref, edge_ref, drand_ref, part_ref,
    stat_ref, ring_ref, mid_ref, plane_ref, ring_send, ring_recv, plane_send, plane_recv,
):
    me, x, z, y = place()
    tp = lax.axis_index("tp")
    peers = plane_peers(x, z, y, tp)
    mine = x * NY + y
    rings = [(offset, (seq_of(x, lax.rem(z + offset, NZ), y), tp)) for offset in range(1, NZ)]
    heads = q_ref.shape[1] // HEAD_DIM

    def head_columns(head):
        return pl.ds(pl.multiple_of(head * HEAD_DIM, HEAD_DIM), HEAD_DIM)

    def gathered(number, columns):
        return gath_ref[:, number, :, columns].reshape(256, HEAD_DIM)

    def global_stats(head, carry):
        columns = head_columns(head)
        scores = nt(k_ref[:, columns], gathered(0, columns)) * SCALE
        slopes = nt(v_ref[:, columns], gathered(3, columns))
        top = jnp.max(scores, axis=0, keepdims=True)
        raised = jnp.exp(scores - top)
        stat_ref[0, pl.ds(head, 1), :] = top
        stat_ref[1, pl.ds(head, 1), :] = jnp.sum(raised, axis=0, keepdims=True)
        stat_ref[2, pl.ds(head, 1), :] = jnp.sum(raised * slopes, axis=0, keepdims=True)
        return carry

    lax.fori_loop(0, heads, global_stats, 0)

    def join(ref):
        top = ref[0, 0]
        for number in range(1, 8):
            top = jnp.maximum(top, ref[number, 0])
        total = jnp.zeros_like(top)
        slope = jnp.zeros_like(top)
        for number in range(8):
            factor = jnp.exp(ref[number, 0] - top)
            total = total + ref[number, 1] * factor
            slope = slope + ref[number, 2] * factor
        return top, total, slope

    greet([peer for _, _, peer in peers] + [peer for _, peer in rings])
    ring_copies = []
    for offset, peer in rings:
        copy = remote(stat_ref, ring_ref.at[offset], ring_send.at[offset], ring_recv.at[offset], peer)
        copy.start()
        ring_copies.append(copy)
    ring_ref[0] = stat_ref[...]

    def sparse(head, carry):
        columns = head_columns(head)
        queries = q_ref[:, columns]
        cots = jnp.where(keep_ref[...] > 0.5, c_ref[:, columns], jnp.zeros((256, HEAD_DIM), BF16))
        keys = jnp.concatenate([k_ref[:, columns], rand_ref[0, :, columns], gathered(1, columns)], axis=0)
        values = jnp.concatenate([v_ref[:, columns], rand_ref[1, :, columns], gathered(2, columns)], axis=0)
        edge_keys = (prev_ref[0, :, columns], next_ref[0, :, columns])
        edge_values = (prev_ref[1, :, columns], next_ref[1, :, columns])
        halves = (queries[:BLK], queries[BLK:])
        cot_halves = (cots[:BLK], cots[BLK:])
        main = nt(keys, queries) * SCALE
        edge = (
            jnp.concatenate([nt(edge_keys[i], halves[i]) for i in range(2)], axis=1) * SCALE + bias_ref[...]
        )
        top = jnp.maximum(jnp.max(main, axis=0, keepdims=True), jnp.max(edge, axis=0, keepdims=True))
        main = jnp.exp(main - top)
        edge = jnp.exp(edge - top)
        inverse = 1.0 / (jnp.sum(main, axis=0, keepdims=True) + jnp.sum(edge, axis=0, keepdims=True))
        main = main * inverse
        edge = edge * inverse
        main_w = main.astype(BF16)
        edge_w = edge.astype(BF16)
        main_g = nt(values, cots)
        edge_g = jnp.concatenate([nt(edge_values[i], cot_halves[i]) for i in range(2)], axis=1)
        delta = jnp.sum(main * main_g, axis=0, keepdims=True) + jnp.sum(edge * edge_g, axis=0, keepdims=True)
        main_s = (main * (main_g - delta) * SCALE).astype(BF16)
        edge_s = (edge * (edge_g - delta) * SCALE).astype(BF16)
        sides = [slice(0, BLK), slice(BLK, 2 * BLK)]
        out = tn(main_w, values) + jnp.concatenate(
            [tn(edge_w[:, sides[i]], edge_values[i]) for i in range(2)], axis=0
        )
        out_ref[:, columns] = out.astype(BF16)
        dq_ref[:, columns] = tn(main_s, keys) + jnp.concatenate(
            [tn(edge_s[:, sides[i]], edge_keys[i]) for i in range(2)], axis=0
        )
        dkeys = nn(main_s, queries)
        dvalues = nn(main_w, cots)
        dk_ref[:, columns] = dkeys[:256]
        dv_ref[:, columns] = dvalues[:256]
        drand_ref[0, :, columns] = dkeys[256:384].astype(BF16)
        drand_ref[1, :, columns] = dvalues[256:384].astype(BF16)
        part_ref[:, 2, :, columns] = dkeys[384:].astype(BF16).reshape(NZ, 32, HEAD_DIM)
        part_ref[:, 3, :, columns] = dvalues[384:].astype(BF16).reshape(NZ, 32, HEAD_DIM)
        for i in range(2):
            edge_ref[i, 0, :, columns] = nn(edge_s[:, sides[i]], halves[i]).astype(BF16)
            edge_ref[i, 1, :, columns] = nn(edge_w[:, sides[i]], cot_halves[i]).astype(BF16)
        return carry

    lax.fori_loop(0, heads // 2, sparse, 0)
    for copy in ring_copies:
        copy.wait()
    for number, value in enumerate(join(ring_ref)):
        mid_ref[number] = value
    plane_ref[0] = mid_ref[...]
    plane_copies = []
    for offset, _, peer in peers:
        copy = remote(mid_ref, plane_ref.at[offset], plane_send.at[offset], plane_recv.at[offset], peer)
        copy.start()
        plane_copies.append(copy)
    lax.fori_loop(heads // 2, heads, sparse, 0)
    for copy in plane_copies:
        copy.wait()
    top, total, slope = join(plane_ref)
    inverse = 1.0 / total
    stat_ref[0] = top
    stat_ref[1] = inverse
    stat_ref[2] = slope * inverse

    def global_grads(head, carry):
        columns = head_columns(head)
        keys, values = k_ref[:, columns], v_ref[:, columns]
        queries, cots = gathered(0, columns), gathered(3, columns)
        row = pl.ds(head, 1)
        probs = jnp.exp(nt(keys, queries) * SCALE - stat_ref[0, row, :]) * stat_ref[1, row, :]
        slopes = nt(values, cots)
        scores = (probs * (slopes - stat_ref[2, row, :]) * SCALE).astype(BF16)
        weights = probs.astype(BF16)
        dk_ref[:, columns] += nn(scores, queries)
        dv_ref[:, columns] += nn(weights, cots)
        part_ref[:, 0, :, columns] = tn(scores, keys).astype(BF16).reshape(NZ, 32, HEAD_DIM)
        part_ref[:, 1, :, columns] = tn(weights, values).astype(BF16).reshape(NZ, 32, HEAD_DIM)
        return carry

    lax.fori_loop(0, heads, global_grads, 0)


def reduce_kernel(
    part_ref, edge_ref, total_ref, first_ref, last_ref,
    out_ring, in_ring, out_piece, in_piece, ring_send, ring_recv, plane_send, plane_recv, edge_send, edge_recv,
):
    me, x, z, y = place()
    tp = lax.axis_index("tp")
    peers = plane_peers(x, z, y, tp)
    right, left = ring_peers(x, z, y, tp)
    after, before = line_peers(me, tp)
    mine = x * NY + y
    greet([peer for _, _, peer in peers] + [right, left, after, before])

    def hop(way, step, number):
        far = steps_of(number)[way] - step + 1
        target = lax.rem(z + far, NZ) if way == 0 else lax.rem(z + NZ - far, NZ)
        slot = (way * 4 + step - 1) * 4 + number
        if step == 1:
            source = part_ref.at[target, number]
        else:
            source = out_ring.at[way, step - 1, number]
            source[...] = (
                part_ref[target, number].astype(F32) + in_ring[way, step - 2, number].astype(F32)
            ).astype(BF16)
        return remote(
            source, in_ring.at[way, step - 1, number], ring_send.at[slot], ring_recv.at[slot],
            right if way == 0 else left,
        )

    flying = {}
    for number in (2, 3, 0, 1):
        for way in range(2):
            flying[way, 1, number] = hop(way, 1, number)
            flying[way, 1, number].start()
    edges = []
    for number in range(2):
        edges.append(
            remote(edge_ref.at[1, number], first_ref.at[number], edge_send.at[number], edge_recv.at[number], after)
        )
        edges.append(
            remote(edge_ref.at[0, number], last_ref.at[number], edge_send.at[2 + number], edge_recv.at[2 + number], before)
        )
    for edge in edges:
        edge.start()
    sums = [None] * 4
    for step in range(1, 5):
        for number in (2, 3, 0, 1):
            for way in range(2):
                if step <= steps_of(number)[way]:
                    flying[way, step, number].wait_recv()
                    if step < steps_of(number)[way]:
                        flying[way, step + 1, number] = hop(way, step + 1, number)
                        flying[way, step + 1, number].start()
    for number in range(4):
        steps = steps_of(number)
        sums[number] = (
            part_ref[z, number].astype(F32)
            + in_ring[0, steps[0] - 1, number].astype(F32)
            + in_ring[1, steps[1] - 1, number].astype(F32)
        ).astype(BF16)
    stacked = jnp.concatenate(sums, axis=0)
    out_row = lax.broadcasted_iota(jnp.int32, (128, 128), 0)
    in_row = lax.broadcasted_iota(jnp.int32, (128, 128), 1)
    source_row = ((out_row % 16) // 4) * 32 + (out_row // 16) * 4 + out_row % 4
    order = jnp.where(in_row == source_row, 1.0, 0.0).astype(BF16)
    out_piece[...] = nn(order, stacked).astype(BF16).reshape(NP, 16, -1)
    copies = []
    for offset, number, peer in peers:
        copy = remote(
            out_piece.at[number], in_piece.at[offset], plane_send.at[offset], plane_recv.at[offset], peer
        )
        copy.start()
        copies.append(copy)
    total = out_piece[mine].astype(F32)
    for copy in copies:
        copy.wait()
    for offset in range(1, NP):
        total = total + in_piece[offset].astype(F32)
    total_ref[...] = total
    for copy in flying.values():
        copy.wait_send()
    for edge in edges:
        edge.wait()


def finish_kernel(
    out_ref, dq_ref, dk_ref, dv_ref, total_ref, first_ref, last_ref, rand_ref, pos_ref, keep_ref, land_ref,
    attention_ref, gq_ref, gk_ref, gv_ref,
):
    rows = lax.broadcasted_iota(jnp.int32, (256, 16), 0)
    columns = lax.broadcasted_iota(jnp.int32, (256, 16), 1)
    hit = rows == pos_ref[...]
    total = total_ref[...]
    high = total.astype(BF16)
    low = (total - high.astype(F32)).astype(BF16)

    def rows_of(number, with_low):
        pick = jnp.where(hit & (columns // 4 == number), 1.0, 0.0).astype(BF16)
        placed = nn(pick, high)
        return placed + nn(pick, low) if with_low else placed

    gq_ref[...] = (dq_ref[...] + rows_of(0, True)).astype(BF16)
    attention_ref[...] = jnp.where(keep_ref[...] > 0.5, out_ref[...], rows_of(1, False).astype(BF16))
    landing = land_ref[...]
    for number, (own_ref, grad_ref) in enumerate(((dk_ref, gk_ref), (dv_ref, gv_ref))):
        back = rand_ref[number].astype(F32)
        edges = jnp.concatenate(
            [first_ref[number].astype(F32), last_ref[number].astype(F32)], axis=0
        )
        borrowed = jnp.concatenate([back, back], axis=0) * landing
        grad_ref[...] = (own_ref[...] + edges + borrowed + rows_of(2 + number, True)).astype(BF16)


VMEM = pl.BlockSpec(memory_space=pltpu.VMEM)
DMA = pltpu.SemaphoreType.DMA


def exchanged(parcel, mask):
    size = lax.axis_size("seq")

    def by(flip):
        return lambda block: lax.ppermute(block, "seq", [(i, i ^ flip) for i in range(size)])

    return lax.switch(mask - 1, [by(flip) for flip in range(1, size)], parcel)


def params(collective_id=None):
    return pltpu.CompilerParams(
        collective_id=collective_id,
        has_side_effects=collective_id is not None,
        vmem_limit_bytes=56 * 1024 * 1024,
    )


def per_device(query_rows, key_rows, value_rows, cotangent, global_pos, partner_mask, rand_block):
    count, columns = query_rows.shape
    me = lax.axis_index("seq")
    shards = lax.axis_size("seq")
    local_pos = global_pos - me * count
    pos_col = jnp.tile(local_pos, 4)[:, None]
    token = jnp.arange(count, dtype=jnp.int32)
    keep = jnp.where(jnp.any(token[:, None] == local_pos[None, :], axis=1, keepdims=True), 0.0, 1.0).astype(F32)
    closed = ((token < BLK) & (me == 0)) | ((token >= BLK) & (me == shards - 1))
    bias = jnp.where(closed, -1e30, 0.0).astype(F32)[None, :]
    chosen = rand_block[0, jnp.bitwise_xor(me, partner_mask[0])]
    landing = jnp.where(token // BLK == chosen, 1.0, 0.0).astype(F32)[:, None]

    def shape(*dims, dtype=BF16):
        return jax.ShapeDtypeStruct(dims, dtype)

    gath, prev, following = pl.pallas_call(
        gather_kernel,
        out_shape=(shape(NZ, 4, 32, columns), shape(2, BLK, columns), shape(2, BLK, columns)),
        in_specs=[VMEM] * 5,
        out_specs=(VMEM,) * 3,
        scratch_shapes=[
            pltpu.VMEM((NP, 16, columns), BF16), DMA((8,)), DMA((8,)), DMA((32,)), DMA((32,)), DMA((4,)), DMA((4,)),
        ],
        compiler_params=params(0),
    )(query_rows, key_rows, value_rows, cotangent, pos_col)

    outgoing = jnp.stack(
        [
            lax.dynamic_slice_in_dim(key_rows, chosen * BLK, BLK, 0),
            lax.dynamic_slice_in_dim(value_rows, chosen * BLK, BLK, 0),
        ]
    )
    borrowed = exchanged(outgoing, partner_mask[0])

    out, dq, dk, dv, edge, drand, part = pl.pallas_call(
        attend_kernel,
        out_shape=(
            shape(count, columns), shape(count, columns, dtype=F32), shape(count, columns, dtype=F32),
            shape(count, columns, dtype=F32), shape(2, 2, BLK, columns), shape(2, BLK, columns),
            shape(NZ, 4, 32, columns),
        ),
        in_specs=[VMEM] * 10,
        out_specs=(VMEM,) * 7,
        scratch_shapes=[
            pltpu.VMEM((3, 8, 256), F32), pltpu.VMEM((8, 3, 8, 256), F32), pltpu.VMEM((3, 8, 256), F32),
            pltpu.VMEM((8, 3, 8, 256), F32), DMA((8,)), DMA((8,)), DMA((8,)), DMA((8,)),
        ],
        compiler_params=params(1),
    )(query_rows, key_rows, value_rows, cotangent, keep, bias, prev, following, borrowed, gath)

    total, first, last = pl.pallas_call(
        reduce_kernel,
        out_shape=(shape(16, columns, dtype=F32), shape(2, BLK, columns), shape(2, BLK, columns)),
        in_specs=[VMEM] * 2,
        out_specs=(VMEM,) * 3,
        scratch_shapes=[
            pltpu.VMEM((2, 4, 4, 32, columns), BF16), pltpu.VMEM((2, 4, 4, 32, columns), BF16),
            pltpu.VMEM((NP, 16, columns), BF16), pltpu.VMEM((NP, 16, columns), BF16),
            DMA((32,)), DMA((32,)), DMA((8,)), DMA((8,)), DMA((4,)), DMA((4,)),
        ],
        compiler_params=params(2),
    )(part, edge)

    returned = exchanged(drand, partner_mask[0])

    width = 256
    wide = lambda *lead: pl.BlockSpec((*lead, width), lambda i: (*([0] * len(lead)), i))
    whole = lambda *dims: pl.BlockSpec(dims, lambda i: (0,) * len(dims))
    return pl.pallas_call(
        finish_kernel,
        grid=(columns // width,),
        out_shape=(shape(count, columns),) * 4,
        in_specs=[
            wide(count), wide(count), wide(count), wide(count), wide(16), wide(2, BLK), wide(2, BLK),
            wide(2, BLK), whole(1, 16), whole(count, 1), whole(count, 1),
        ],
        out_specs=(wide(count),) * 4,
        compiler_params=params(),
    )(out, dq, dk, dv, total, first, last, returned, pos_col.reshape(1, 16), keep, landing)


def solution(mesh):
    placed = (P("seq", "tp"),) * 4 + (P("seq"), P(), P())
    return jax.shard_map(
        per_device,
        mesh=mesh,
        in_specs=placed,
        out_specs=(P("seq", "tp"),) * 4,
        check_vma=False,
    )
```

```python
import functools

import jax
import jax.numpy as jnp
from jax import lax
from jax.experimental import pallas as pl
from jax.experimental.pallas import tpu as pltpu
from jax.sharding import PartitionSpec as P

HEAD_DIM = 128
BLK = 128
NX, NZ, NY = 2, 8, 4
NP = NX * NY
SCALE = HEAD_DIM**-0.5
MESH = pl.DeviceIdType.MESH
F32 = jnp.float32
BF16 = jnp.bfloat16


def nt(a, b):
    return lax.dot_general(a, b, (((1,), (1,)), ((), ())), preferred_element_type=F32)


def nn(a, b):
    return lax.dot_general(a, b, (((1,), (0,)), ((), ())), preferred_element_type=F32)


def tn(a, b):
    return lax.dot_general(a, b, (((0,), (0,)), ((), ())), preferred_element_type=F32)


def place():
    me = lax.axis_index("seq")
    return me, me // (NZ * NY), (me // NY) % NZ, me % NY


def seq_of(x, z, y):
    return (x * NZ + z) * NY + y


def greet(peers):
    barrier = pltpu.get_barrier_semaphore()
    for peer in peers:
        pl.semaphore_signal(barrier, inc=1, device_id=peer, device_id_type=MESH)
    pl.semaphore_wait(barrier, len(peers))


def plane_peers(x, z, y, tp):
    peers = []
    for offset in range(1, NP):
        dx, dy = offset // NY, offset % NY
        px, py = lax.rem(x + dx, NX), lax.rem(y + dy, NY)
        peers.append((offset, px * NY + py, (seq_of(px, z, py), tp)))
    return peers


def ring_peers(x, z, y, tp):
    return (seq_of(x, lax.rem(z + 1, NZ), y), tp), (seq_of(x, lax.rem(z + NZ - 1, NZ), y), tp)


def flipped(value, flip):
    bit = 1
    while bit <= flip:
        if flip & bit:
            value = value + bit * (1 - 2 * ((value // bit) % 2))
        bit *= 2
    return value


def line_peers(me, tp):
    return (lax.rem(me + 1, NX * NZ * NY), tp), (lax.rem(me + NX * NZ * NY - 1, NX * NZ * NY), tp)


def remote(src, dst, send, recv, device):
    return pltpu.make_async_remote_copy(
        src_ref=src, dst_ref=dst, send_sem=send, recv_sem=recv, device_id=device, device_id_type=MESH
    )


def swap_in_plane(flip, x, z, y, tp, source, target, send, recv):
    if flip == 0:
        target[...] = source[...]
        return []
    device = (seq_of(flipped(x, flip // NY), z, flipped(y, flip % NY)), tp)
    swaps = [
        remote(source.at[number], target.at[number], send.at[number], recv.at[number], device)
        for number in range(2)
    ]
    for swap in swaps:
        swap.start()
    return swaps


def steps_of(array):
    return (4, 3) if array < 2 else (3, 4)


def gather_kernel(
    flip, q_ref, k_ref, v_ref, c_ref, pos_ref, parcel_ref, gath_ref, passed_ref,
    piece_ref, plane_send, plane_recv, ring_send, ring_recv, swap_send, swap_recv,
):
    me, x, z, y = place()
    tp = lax.axis_index("tp")
    peers = plane_peers(x, z, y, tp)
    right, left = ring_peers(x, z, y, tp)
    mine = x * NY + y

    rows = lax.broadcasted_iota(jnp.int32, (16, 256), 0)
    columns = lax.broadcasted_iota(jnp.int32, (16, 256), 1)
    hit = columns == pos_ref[...]
    total = jnp.zeros((16, q_ref.shape[1]), F32)
    for number, ref in enumerate((q_ref, k_ref, v_ref, c_ref)):
        pick = jnp.where(hit & (rows // 4 == number), 1.0, 0.0).astype(BF16)
        total = total + nn(pick, ref[...])
    piece_ref[mine] = total.astype(BF16)

    greet([peer for _, _, peer in peers] + [right, left])
    copies = []
    for offset, _, peer in peers:
        copy = remote(
            piece_ref.at[mine], piece_ref.at[mine], plane_send.at[offset], plane_recv.at[offset], peer
        )
        copy.start()
        copies.append(copy)
    swaps = swap_in_plane(flip, x, z, y, tp, parcel_ref, passed_ref, swap_send, swap_recv)
    for copy in copies:
        copy.wait()

    out_row = lax.broadcasted_iota(jnp.int32, (32, 128), 0)
    in_row = lax.broadcasted_iota(jnp.int32, (32, 128), 1)
    pieces = piece_ref[...].reshape(128, -1)
    for number in range(4):
        pick = jnp.where(in_row == (out_row // 4) * 16 + number * 4 + out_row % 4, 1.0, 0.0)
        gath_ref[z, number] = nn(pick.astype(BF16), pieces).astype(BF16)

    def hop(way, step, number):
        shift = lax.rem(z + NZ - step + 1, NZ) if way == 0 else lax.rem(z + step - 1, NZ)
        slot = (way * 4 + step - 1) * 4 + number
        part = gath_ref.at[shift, number]
        return remote(part, part, ring_send.at[slot], ring_recv.at[slot], right if way == 0 else left)

    flying = {}
    for number in range(4):
        for way in range(2):
            flying[way, 1, number] = hop(way, 1, number)
            flying[way, 1, number].start()
    for step in range(1, 5):
        for number in range(4):
            for way in range(2):
                if step <= steps_of(number)[way]:
                    flying[way, step, number].wait_recv()
                    if step < steps_of(number)[way]:
                        flying[way, step + 1, number] = hop(way, step + 1, number)
                        flying[way, step + 1, number].start()
    for copy in flying.values():
        copy.wait_send()
    for swap in swaps:
        swap.wait()


def attend_kernel(
    flip, q_ref, k_ref, v_ref, c_ref, keep_ref, bias_ref, passed_ref, gath_ref,
    out_ref, dq_ref, dk_ref, dv_ref, first_ref, last_ref, back_ref, part_ref,
    stat_ref, ring_ref, mid_ref, plane_ref, prev_ref, next_ref, edge_ref, far_ref, near_ref,
    ring_send, ring_recv, plane_send, plane_recv, edge_send, edge_recv, swap_send, swap_recv,
):
    me, x, z, y = place()
    tp = lax.axis_index("tp")
    peers = plane_peers(x, z, y, tp)
    mine = x * NY + y
    rings = [(offset, (seq_of(x, lax.rem(z + offset, NZ), y), tp)) for offset in range(1, NZ)]
    heads = q_ref.shape[1] // HEAD_DIM
    after, before = line_peers(me, tp)
    rand_ref, drand_ref = (far_ref, near_ref) if flip else (passed_ref, back_ref)
    partner = (seq_of(x, flipped(z, flip), y), tp)

    greet([peer for _, _, peer in peers] + [peer for _, peer in rings] + [after, before])
    swaps = [
        remote(passed_ref.at[i], far_ref.at[i], swap_send.at[i], swap_recv.at[i], partner)
        for i in range(2 if flip else 0)
    ]
    for number, ref in enumerate((k_ref, v_ref)):
        swaps.append(
            remote(ref.at[pl.ds(BLK, BLK)], prev_ref.at[number], edge_send.at[number], edge_recv.at[number], after)
        )
        swaps.append(
            remote(ref.at[pl.ds(0, BLK)], next_ref.at[number], edge_send.at[2 + number], edge_recv.at[2 + number], before)
        )
    for swap in swaps:
        swap.start()

    def head_columns(head):
        return pl.ds(pl.multiple_of(head * HEAD_DIM, HEAD_DIM), HEAD_DIM)

    def gathered(number, columns):
        return gath_ref[:, number, :, columns].reshape(256, HEAD_DIM)

    def global_stats(head, carry):
        columns = head_columns(head)
        scores = nt(k_ref[:, columns], gathered(0, columns)) * SCALE
        slopes = nt(v_ref[:, columns], gathered(3, columns))
        top = jnp.max(scores, axis=0, keepdims=True)
        raised = jnp.exp(scores - top)
        stat_ref[0, pl.ds(head, 1), :] = top
        stat_ref[1, pl.ds(head, 1), :] = jnp.sum(raised, axis=0, keepdims=True)
        stat_ref[2, pl.ds(head, 1), :] = jnp.sum(raised * slopes, axis=0, keepdims=True)
        return carry

    lax.fori_loop(0, heads, global_stats, 0)

    def join(ref):
        top = ref[0, 0]
        for number in range(1, 8):
            top = jnp.maximum(top, ref[number, 0])
        total = jnp.zeros_like(top)
        slope = jnp.zeros_like(top)
        for number in range(8):
            factor = jnp.exp(ref[number, 0] - top)
            total = total + ref[number, 1] * factor
            slope = slope + ref[number, 2] * factor
        return top, total, slope

    ring_copies = []
    for offset, peer in rings:
        copy = remote(stat_ref, ring_ref.at[offset], ring_send.at[offset], ring_recv.at[offset], peer)
        copy.start()
        ring_copies.append(copy)
    ring_ref[0] = stat_ref[...]

    def sparse(head, carry):
        columns = head_columns(head)
        queries = q_ref[:, columns]
        cots = jnp.where(keep_ref[...] > 0.5, c_ref[:, columns], jnp.zeros((256, HEAD_DIM), BF16))
        keys = jnp.concatenate([k_ref[:, columns], rand_ref[0, :, columns], gathered(1, columns)], axis=0)
        values = jnp.concatenate([v_ref[:, columns], rand_ref[1, :, columns], gathered(2, columns)], axis=0)
        edge_keys = (prev_ref[0, :, columns], next_ref[0, :, columns])
        edge_values = (prev_ref[1, :, columns], next_ref[1, :, columns])
        halves = (queries[:BLK], queries[BLK:])
        cot_halves = (cots[:BLK], cots[BLK:])
        main = nt(keys, queries) * SCALE
        edge = (
            jnp.concatenate([nt(edge_keys[i], halves[i]) for i in range(2)], axis=1) * SCALE + bias_ref[...]
        )
        top = jnp.maximum(jnp.max(main, axis=0, keepdims=True), jnp.max(edge, axis=0, keepdims=True))
        main = jnp.exp(main - top)
        edge = jnp.exp(edge - top)
        inverse = 1.0 / (jnp.sum(main, axis=0, keepdims=True) + jnp.sum(edge, axis=0, keepdims=True))
        main = main * inverse
        edge = edge * inverse
        main_w = main.astype(BF16)
        edge_w = edge.astype(BF16)
        main_g = nt(values, cots)
        edge_g = jnp.concatenate([nt(edge_values[i], cot_halves[i]) for i in range(2)], axis=1)
        delta = jnp.sum(main * main_g, axis=0, keepdims=True) + jnp.sum(edge * edge_g, axis=0, keepdims=True)
        main_s = (main * (main_g - delta) * SCALE).astype(BF16)
        edge_s = (edge * (edge_g - delta) * SCALE).astype(BF16)
        sides = [slice(0, BLK), slice(BLK, 2 * BLK)]
        out = tn(main_w, values) + jnp.concatenate(
            [tn(edge_w[:, sides[i]], edge_values[i]) for i in range(2)], axis=0
        )
        out_ref[:, columns] = out.astype(BF16)
        dq_ref[:, columns] = tn(main_s, keys) + jnp.concatenate(
            [tn(edge_s[:, sides[i]], edge_keys[i]) for i in range(2)], axis=0
        )
        dkeys = nn(main_s, queries)
        dvalues = nn(main_w, cots)
        dk_ref[:, columns] = dkeys[:256]
        dv_ref[:, columns] = dvalues[:256]
        drand_ref[0, :, columns] = dkeys[256:384].astype(BF16)
        drand_ref[1, :, columns] = dvalues[256:384].astype(BF16)
        part_ref[:, 2, :, columns] = dkeys[384:].astype(BF16).reshape(NZ, 32, HEAD_DIM)
        part_ref[:, 3, :, columns] = dvalues[384:].astype(BF16).reshape(NZ, 32, HEAD_DIM)
        for i in range(2):
            edge_ref[i, 0, :, columns] = nn(edge_s[:, sides[i]], halves[i]).astype(BF16)
            edge_ref[i, 1, :, columns] = nn(edge_w[:, sides[i]], cot_halves[i]).astype(BF16)
        return carry

    for swap in swaps:
        swap.wait()
    lax.fori_loop(0, heads // 2, sparse, 0)
    for copy in ring_copies:
        copy.wait()
    for number, value in enumerate(join(ring_ref)):
        mid_ref[number] = value
    plane_ref[0] = mid_ref[...]
    plane_copies = []
    for offset, _, peer in peers:
        copy = remote(mid_ref, plane_ref.at[offset], plane_send.at[offset], plane_recv.at[offset], peer)
        copy.start()
        plane_copies.append(copy)
    lax.fori_loop(heads // 2, heads, sparse, 0)
    returns = [
        remote(near_ref.at[i], back_ref.at[i], swap_send.at[2 + i], swap_recv.at[2 + i], partner)
        for i in range(2 if flip else 0)
    ]
    for number in range(2):
        returns.append(
            remote(edge_ref.at[1, number], first_ref.at[number], edge_send.at[4 + number], edge_recv.at[4 + number], after)
        )
        returns.append(
            remote(edge_ref.at[0, number], last_ref.at[number], edge_send.at[6 + number], edge_recv.at[6 + number], before)
        )
    for copy in returns:
        copy.start()
    for copy in plane_copies:
        copy.wait()
    top, total, slope = join(plane_ref)
    inverse = 1.0 / total
    stat_ref[0] = top
    stat_ref[1] = inverse
    stat_ref[2] = slope * inverse

    def global_grads(head, carry):
        columns = head_columns(head)
        keys, values = k_ref[:, columns], v_ref[:, columns]
        queries, cots = gathered(0, columns), gathered(3, columns)
        row = pl.ds(head, 1)
        probs = jnp.exp(nt(keys, queries) * SCALE - stat_ref[0, row, :]) * stat_ref[1, row, :]
        slopes = nt(values, cots)
        scores = (probs * (slopes - stat_ref[2, row, :]) * SCALE).astype(BF16)
        weights = probs.astype(BF16)
        dk_ref[:, columns] += nn(scores, queries)
        dv_ref[:, columns] += nn(weights, cots)
        part_ref[:, 0, :, columns] = tn(scores, keys).astype(BF16).reshape(NZ, 32, HEAD_DIM)
        part_ref[:, 1, :, columns] = tn(weights, values).astype(BF16).reshape(NZ, 32, HEAD_DIM)
        return carry

    lax.fori_loop(0, heads, global_grads, 0)
    for copy in returns:
        copy.wait()


def reduce_kernel(
    flip, part_ref, back_ref, total_ref, home_ref,
    out_ring, in_ring, out_piece, in_piece, ring_send, ring_recv, plane_send, plane_recv, swap_send, swap_recv,
):
    me, x, z, y = place()
    tp = lax.axis_index("tp")
    peers = plane_peers(x, z, y, tp)
    right, left = ring_peers(x, z, y, tp)
    mine = x * NY + y
    greet([peer for _, _, peer in peers] + [right, left])

    def hop(way, step, number):
        far = steps_of(number)[way] - step + 1
        target = lax.rem(z + far, NZ) if way == 0 else lax.rem(z + NZ - far, NZ)
        slot = (way * 4 + step - 1) * 4 + number
        if step == 1:
            source = part_ref.at[target, number]
        else:
            source = out_ring.at[way, step - 1, number]
            source[...] = (
                part_ref[target, number].astype(F32) + in_ring[way, step - 2, number].astype(F32)
            ).astype(BF16)
        return remote(
            source, in_ring.at[way, step - 1, number], ring_send.at[slot], ring_recv.at[slot],
            right if way == 0 else left,
        )

    flying = {}
    for number in (2, 3, 0, 1):
        for way in range(2):
            flying[way, 1, number] = hop(way, 1, number)
            flying[way, 1, number].start()
    swaps = swap_in_plane(flip, x, z, y, tp, back_ref, home_ref, swap_send, swap_recv)
    sums = [None] * 4
    for step in range(1, 5):
        for number in (2, 3, 0, 1):
            for way in range(2):
                if step <= steps_of(number)[way]:
                    flying[way, step, number].wait_recv()
                    if step < steps_of(number)[way]:
                        flying[way, step + 1, number] = hop(way, step + 1, number)
                        flying[way, step + 1, number].start()
    for number in range(4):
        steps = steps_of(number)
        sums[number] = (
            part_ref[z, number].astype(F32)
            + in_ring[0, steps[0] - 1, number].astype(F32)
            + in_ring[1, steps[1] - 1, number].astype(F32)
        ).astype(BF16)
    stacked = jnp.concatenate(sums, axis=0)
    out_row = lax.broadcasted_iota(jnp.int32, (128, 128), 0)
    in_row = lax.broadcasted_iota(jnp.int32, (128, 128), 1)
    source_row = ((out_row % 16) // 4) * 32 + (out_row // 16) * 4 + out_row % 4
    order = jnp.where(in_row == source_row, 1.0, 0.0).astype(BF16)
    out_piece[...] = nn(order, stacked).astype(BF16).reshape(NP, 16, -1)
    copies = []
    for offset, number, peer in peers:
        copy = remote(
            out_piece.at[number], in_piece.at[offset], plane_send.at[offset], plane_recv.at[offset], peer
        )
        copy.start()
        copies.append(copy)
    total = out_piece[mine].astype(F32)
    for copy in copies:
        copy.wait()
    for offset in range(1, NP):
        total = total + in_piece[offset].astype(F32)
    total_ref[...] = total
    for copy in flying.values():
        copy.wait_send()
    for swap in swaps:
        swap.wait()


def finish_kernel(
    out_ref, dq_ref, dk_ref, dv_ref, total_ref, first_ref, last_ref, rand_ref, pos_ref, keep_ref, land_ref,
    attention_ref, gq_ref, gk_ref, gv_ref,
):
    rows = lax.broadcasted_iota(jnp.int32, (256, 16), 0)
    columns = lax.broadcasted_iota(jnp.int32, (256, 16), 1)
    hit = rows == pos_ref[...]
    total = total_ref[...]
    high = total.astype(BF16)
    low = (total - high.astype(F32)).astype(BF16)

    def rows_of(number, with_low):
        pick = jnp.where(hit & (columns // 4 == number), 1.0, 0.0).astype(BF16)
        placed = nn(pick, high)
        return placed + nn(pick, low) if with_low else placed

    gq_ref[...] = (dq_ref[...] + rows_of(0, True)).astype(BF16)
    attention_ref[...] = jnp.where(keep_ref[...] > 0.5, out_ref[...], rows_of(1, False).astype(BF16))
    landing = land_ref[...]
    for number, (own_ref, grad_ref) in enumerate(((dk_ref, gk_ref), (dv_ref, gv_ref))):
        back = rand_ref[number].astype(F32)
        edges = jnp.concatenate(
            [first_ref[number].astype(F32), last_ref[number].astype(F32)], axis=0
        )
        borrowed = jnp.concatenate([back, back], axis=0) * landing
        grad_ref[...] = (own_ref[...] + edges + borrowed + rows_of(2 + number, True)).astype(BF16)


VMEM = pl.BlockSpec(memory_space=pltpu.VMEM)
DMA = pltpu.SemaphoreType.DMA


def params(collective_id=None):
    return pltpu.CompilerParams(
        collective_id=collective_id,
        has_side_effects=collective_id is not None,
        vmem_limit_bytes=56 * 1024 * 1024,
    )


def per_device(query_rows, key_rows, value_rows, cotangent, global_pos, partner_mask, rand_block):
    count, columns = query_rows.shape
    me = lax.axis_index("seq")
    shards = lax.axis_size("seq")
    local_pos = global_pos - me * count
    pos_col = jnp.tile(local_pos, 4)[:, None]
    token = jnp.arange(count, dtype=jnp.int32)
    keep = jnp.where(jnp.any(token[:, None] == local_pos[None, :], axis=1, keepdims=True), 0.0, 1.0).astype(F32)
    closed = ((token < BLK) & (me == 0)) | ((token >= BLK) & (me == shards - 1))
    bias = jnp.where(closed, -1e30, 0.0).astype(F32)[None, :]
    chosen = rand_block[0, jnp.bitwise_xor(me, partner_mask[0])]
    landing = jnp.where(token // BLK == chosen, 1.0, 0.0).astype(F32)[:, None]

    def shape(*dims, dtype=BF16):
        return jax.ShapeDtypeStruct(dims, dtype)

    outgoing = jnp.stack(
        [
            lax.dynamic_slice_in_dim(key_rows, chosen * BLK, BLK, 0),
            lax.dynamic_slice_in_dim(value_rows, chosen * BLK, BLK, 0),
        ]
    )
    mask = partner_mask[0]
    in_plane = jnp.right_shift(mask, 5) * NY + jnp.bitwise_and(mask, 3)
    along_z = jnp.bitwise_and(jnp.right_shift(mask, 2), 7)

    def chosen_by(index, build, *operands):
        return lax.switch(index, [build(flip) for flip in range(8)], *operands)

    def gather(flip):
        return pl.pallas_call(
            functools.partial(gather_kernel, flip),
            out_shape=(shape(NZ, 4, 32, columns), shape(2, BLK, columns)),
            in_specs=[VMEM] * 6,
            out_specs=(VMEM,) * 2,
            scratch_shapes=[
                pltpu.VMEM((NP, 16, columns), BF16), DMA((8,)), DMA((8,)), DMA((32,)), DMA((32,)), DMA((2,)), DMA((2,)),
            ],
            compiler_params=params(flip),
        )

    gath, passed = chosen_by(
        in_plane, gather, query_rows, key_rows, value_rows, cotangent, pos_col, outgoing
    )

    def attend(flip):
        stat, stats = pltpu.VMEM((3, 8, 256), F32), pltpu.VMEM((8, 3, 8, 256), F32)
        pair = pltpu.VMEM((2, BLK, columns), BF16)
        return pl.pallas_call(
            functools.partial(attend_kernel, flip),
            out_shape=(
                shape(count, columns), shape(count, columns, dtype=F32), shape(count, columns, dtype=F32),
                shape(count, columns, dtype=F32), shape(2, BLK, columns), shape(2, BLK, columns),
                shape(2, BLK, columns), shape(NZ, 4, 32, columns),
            ),
            in_specs=[VMEM] * 8,
            out_specs=(VMEM,) * 8,
            scratch_shapes=[
                stat, stats, stat, stats, pair, pair, pltpu.VMEM((2, 2, BLK, columns), BF16), pair, pair,
                DMA((8,)), DMA((8,)), DMA((8,)), DMA((8,)), DMA((8,)), DMA((8,)), DMA((4,)), DMA((4,)),
            ],
            compiler_params=params(8 + flip),
        )

    out, dq, dk, dv, first, last, back, part = chosen_by(
        along_z, attend, query_rows, key_rows, value_rows, cotangent, keep, bias, passed, gath
    )

    def reduce(flip):
        return pl.pallas_call(
            functools.partial(reduce_kernel, flip),
            out_shape=(shape(16, columns, dtype=F32), shape(2, BLK, columns)),
            in_specs=[VMEM] * 2,
            out_specs=(VMEM,) * 2,
            scratch_shapes=[
                pltpu.VMEM((2, 4, 4, 32, columns), BF16), pltpu.VMEM((2, 4, 4, 32, columns), BF16),
                pltpu.VMEM((NP, 16, columns), BF16), pltpu.VMEM((NP, 16, columns), BF16),
                DMA((32,)), DMA((32,)), DMA((8,)), DMA((8,)), DMA((2,)), DMA((2,)),
            ],
            compiler_params=params(16 + flip),
        )

    total, returned = chosen_by(in_plane, reduce, part, back)

    width = 256
    wide = lambda *lead: pl.BlockSpec((*lead, width), lambda i: (*([0] * len(lead)), i))
    whole = lambda *dims: pl.BlockSpec(dims, lambda i: (0,) * len(dims))
    return pl.pallas_call(
        finish_kernel,
        grid=(columns // width,),
        out_shape=(shape(count, columns),) * 4,
        in_specs=[
            wide(count), wide(count), wide(count), wide(count), wide(16), wide(2, BLK), wide(2, BLK),
            wide(2, BLK), whole(1, 16), whole(count, 1), whole(count, 1),
        ],
        out_specs=(wide(count),) * 4,
        compiler_params=params(),
    )(out, dq, dk, dv, total, first, last, returned, pos_col.reshape(1, 16), keep, landing)


def solution(mesh):
    placed = (P("seq", "tp"),) * 4 + (P("seq"), P(), P())
    return jax.shard_map(
        per_device,
        mesh=mesh,
        in_specs=placed,
        out_specs=(P("seq", "tp"),) * 4,
        check_vma=False,
    )
```

```python
import functools

import jax
import jax.numpy as jnp
from jax import lax
from jax.experimental import pallas as pl
from jax.experimental.pallas import tpu as pltpu
from jax.sharding import PartitionSpec as P

HEAD_DIM = 128
BLK = 128
NX, NZ, NY = 2, 8, 4
NP = NX * NY
SCALE = HEAD_DIM**-0.5
MESH = pl.DeviceIdType.MESH
F32 = jnp.float32
BF16 = jnp.bfloat16


def nt(a, b):
    return lax.dot_general(a, b, (((1,), (1,)), ((), ())), preferred_element_type=F32)


def nn(a, b):
    return lax.dot_general(a, b, (((1,), (0,)), ((), ())), preferred_element_type=F32)


def tn(a, b):
    return lax.dot_general(a, b, (((0,), (0,)), ((), ())), preferred_element_type=F32)


def place():
    me = lax.axis_index("seq")
    return me, me // (NZ * NY), (me // NY) % NZ, me % NY


def seq_of(x, z, y):
    return (x * NZ + z) * NY + y


def greet(peers):
    barrier = pltpu.get_barrier_semaphore()
    for peer in peers:
        pl.semaphore_signal(barrier, inc=1, device_id=peer, device_id_type=MESH)
    pl.semaphore_wait(barrier, len(peers))


def plane_peers(x, z, y, tp):
    peers = []
    for offset in range(1, NP):
        dx, dy = offset // NY, offset % NY
        px, py = lax.rem(x + dx, NX), lax.rem(y + dy, NY)
        peers.append((offset, px * NY + py, (seq_of(px, z, py), tp)))
    return peers


def ring_peers(x, z, y, tp):
    return (seq_of(x, lax.rem(z + 1, NZ), y), tp), (seq_of(x, lax.rem(z + NZ - 1, NZ), y), tp)


def flipped(value, flip):
    bit = 1
    while bit <= flip:
        if flip & bit:
            value = value + bit * (1 - 2 * ((value // bit) % 2))
        bit *= 2
    return value


def line_peers(me, tp):
    return (lax.rem(me + 1, NX * NZ * NY), tp), (lax.rem(me + NX * NZ * NY - 1, NX * NZ * NY), tp)


def remote(src, dst, send, recv, device):
    return pltpu.make_async_remote_copy(
        src_ref=src, dst_ref=dst, send_sem=send, recv_sem=recv, device_id=device, device_id_type=MESH
    )


def position_of(info_ref, rows):
    turn = rows % 4
    found = jnp.where(turn == 0, info_ref[0], info_ref[1])
    return jnp.where(turn == 2, info_ref[2], jnp.where(turn == 3, info_ref[3], found))


def is_global(info_ref, shape, dimension):
    token = lax.broadcasted_iota(jnp.int32, shape, dimension)
    hit = token == info_ref[0]
    for number in range(1, 4):
        hit = hit | (token == info_ref[number])
    return hit


def head_columns(head):
    return pl.ds(pl.multiple_of(head * HEAD_DIM, HEAD_DIM), HEAD_DIM)


def swap_in_plane(flip, x, z, y, tp, source, target, send, recv):
    if flip == 0:
        return []
    device = (seq_of(flipped(x, flip // NY), z, flipped(y, flip % NY)), tp)
    swaps = [
        remote(source.at[number], target.at[number], send.at[number], recv.at[number], device)
        for number in range(2)
    ]
    for swap in swaps:
        swap.start()
    return swaps


def steps_of(array):
    return (4, 3) if array < 2 else (3, 4)


def gather_kernel(
    flip, info_ref, q_ref, k_ref, v_ref, c_ref, gath_ref, passed_ref,
    parcel_ref, piece_ref, plane_send, plane_recv, ring_send, ring_recv, swap_send, swap_recv,
):
    me, x, z, y = place()
    tp = lax.axis_index("tp")
    peers = plane_peers(x, z, y, tp)
    right, left = ring_peers(x, z, y, tp)
    mine = x * NY + y

    rows = lax.broadcasted_iota(jnp.int32, (16, 256), 0)
    columns = lax.broadcasted_iota(jnp.int32, (16, 256), 1)
    hit = columns == position_of(info_ref, rows)
    total = jnp.zeros((16, q_ref.shape[1]), F32)
    for number, ref in enumerate((q_ref, k_ref, v_ref, c_ref)):
        pick = jnp.where(hit & (rows // 4 == number), 1.0, 0.0).astype(BF16)
        total = total + nn(pick, ref[...])
    piece_ref[mine] = total.astype(BF16)
    target = parcel_ref if flip else passed_ref
    for number, ref in enumerate((k_ref, v_ref)):
        target[number] = jnp.where(info_ref[4] == 1, ref[BLK:], ref[:BLK])

    greet([peer for _, _, peer in peers] + [right, left])
    copies = []
    for offset, _, peer in peers:
        copy = remote(
            piece_ref.at[mine], piece_ref.at[mine], plane_send.at[offset], plane_recv.at[offset], peer
        )
        copy.start()
        copies.append(copy)
    swaps = swap_in_plane(flip, x, z, y, tp, parcel_ref, passed_ref, swap_send, swap_recv)
    for copy in copies:
        copy.wait()

    out_row = lax.broadcasted_iota(jnp.int32, (32, 128), 0)
    in_row = lax.broadcasted_iota(jnp.int32, (32, 128), 1)
    pieces = piece_ref[...].reshape(128, -1)
    for number in range(4):
        pick = jnp.where(in_row == (out_row // 4) * 16 + number * 4 + out_row % 4, 1.0, 0.0)
        gath_ref[z, number] = nn(pick.astype(BF16), pieces).astype(BF16)

    def hop(way, step, number):
        shift = lax.rem(z + NZ - step + 1, NZ) if way == 0 else lax.rem(z + step - 1, NZ)
        slot = (way * 4 + step - 1) * 4 + number
        part = gath_ref.at[shift, number]
        return remote(part, part, ring_send.at[slot], ring_recv.at[slot], right if way == 0 else left)

    flying = {}
    for number in range(4):
        for way in range(2):
            flying[way, 1, number] = hop(way, 1, number)
            flying[way, 1, number].start()
    for step in range(1, 5):
        for number in range(4):
            for way in range(2):
                if step <= steps_of(number)[way]:
                    flying[way, step, number].wait_recv()
                    if step < steps_of(number)[way]:
                        flying[way, step + 1, number] = hop(way, step + 1, number)
                        flying[way, step + 1, number].start()
    for copy in flying.values():
        copy.wait_send()
    for swap in swaps:
        swap.wait()


def join(ref):
    top = ref[0, 0]
    for number in range(1, 8):
        top = jnp.maximum(top, ref[number, 0])
    total = jnp.zeros_like(top)
    slope = jnp.zeros_like(top)
    for number in range(8):
        factor = jnp.exp(ref[number, 0] - top)
        total = total + ref[number, 1] * factor
        slope = slope + ref[number, 2] * factor
    return top, total, slope


def stats_kernel(
    flip, k_ref, v_ref, passed_ref, gath_ref, prev_ref, next_ref, rand_ref, final_ref,
    stat_ref, ring_ref, mid_ref, plane_ref,
    ring_send, ring_recv, plane_send, plane_recv, edge_send, edge_recv, swap_send, swap_recv,
):
    me, x, z, y = place()
    tp = lax.axis_index("tp")
    peers = plane_peers(x, z, y, tp)
    rings = [(offset, (seq_of(x, lax.rem(z + offset, NZ), y), tp)) for offset in range(1, NZ)]
    heads = k_ref.shape[1] // HEAD_DIM
    after, before = line_peers(me, tp)
    partner = (seq_of(x, flipped(z, flip), y), tp)

    greet([peer for _, _, peer in peers] + [peer for _, peer in rings] + [after, before])
    swaps = [
        remote(passed_ref.at[i], rand_ref.at[i], swap_send.at[i], swap_recv.at[i], partner)
        for i in range(2 if flip else 0)
    ]
    for number, ref in enumerate((k_ref, v_ref)):
        swaps.append(
            remote(ref.at[pl.ds(BLK, BLK)], prev_ref.at[number], edge_send.at[number], edge_recv.at[number], after)
        )
        swaps.append(
            remote(ref.at[pl.ds(0, BLK)], next_ref.at[number], edge_send.at[2 + number], edge_recv.at[2 + number], before)
        )
    for swap in swaps:
        swap.start()
    if flip == 0:
        rand_ref[...] = passed_ref[...]

    def global_stats(head, carry):
        columns = head_columns(head)
        queries = gath_ref[:, 0, :, columns].reshape(256, HEAD_DIM)
        cots = gath_ref[:, 3, :, columns].reshape(256, HEAD_DIM)
        scores = nt(k_ref[:, columns], queries) * SCALE
        slopes = nt(v_ref[:, columns], cots)
        top = jnp.max(scores, axis=0, keepdims=True)
        raised = jnp.exp(scores - top)
        stat_ref[0, pl.ds(head, 1), :] = top
        stat_ref[1, pl.ds(head, 1), :] = jnp.sum(raised, axis=0, keepdims=True)
        stat_ref[2, pl.ds(head, 1), :] = jnp.sum(raised * slopes, axis=0, keepdims=True)
        return carry

    lax.fori_loop(0, heads, global_stats, 0)
    ring_copies = []
    for offset, peer in rings:
        copy = remote(stat_ref, ring_ref.at[offset], ring_send.at[offset], ring_recv.at[offset], peer)
        copy.start()
        ring_copies.append(copy)
    ring_ref[0] = stat_ref[...]
    for copy in ring_copies:
        copy.wait()
    for number, value in enumerate(join(ring_ref)):
        mid_ref[number] = value
    plane_copies = []
    for offset, _, peer in peers:
        copy = remote(mid_ref, plane_ref.at[offset], plane_send.at[offset], plane_recv.at[offset], peer)
        copy.start()
        plane_copies.append(copy)
    plane_ref[0] = mid_ref[...]
    for copy in plane_copies:
        copy.wait()
    top, total, slope = join(plane_ref)
    inverse = 1.0 / total
    final_ref[0] = top
    final_ref[1] = inverse
    final_ref[2] = slope * inverse
    for swap in swaps:
        swap.wait()


def attend_kernel(
    info_ref, q_ref, k_ref, v_ref, c_ref, prev_ref, next_ref, rand_ref, gath_ref,
    out_ref, dq_ref, dk_ref, dv_ref, drand_ref, edge_ref, part_ref,
):
    queries = q_ref[...]
    hit = is_global(info_ref, (256, HEAD_DIM), 0)
    cots = jnp.where(hit, jnp.zeros((256, HEAD_DIM), BF16), c_ref[...])
    keys = jnp.concatenate([k_ref[...], rand_ref[0], gath_ref[:, 1].reshape(256, HEAD_DIM)], axis=0)
    values = jnp.concatenate([v_ref[...], rand_ref[1], gath_ref[:, 2].reshape(256, HEAD_DIM)], axis=0)
    edge_keys = (prev_ref[0], next_ref[0])
    edge_values = (prev_ref[1], next_ref[1])
    halves = (queries[:BLK], queries[BLK:])
    cot_halves = (cots[:BLK], cots[BLK:])
    token = lax.broadcasted_iota(jnp.int32, (1, 2 * BLK), 1)
    closed = ((token < BLK) & (info_ref[5] == 0)) | ((token >= BLK) & (info_ref[5] == NX * NZ * NY - 1))
    bias = jnp.where(closed, -1e30, 0.0)
    main = nt(keys, queries) * SCALE
    edge = jnp.concatenate([nt(edge_keys[i], halves[i]) for i in range(2)], axis=1) * SCALE + bias
    top = jnp.maximum(jnp.max(main, axis=0, keepdims=True), jnp.max(edge, axis=0, keepdims=True))
    main = jnp.exp(main - top)
    edge = jnp.exp(edge - top)
    inverse = 1.0 / (jnp.sum(main, axis=0, keepdims=True) + jnp.sum(edge, axis=0, keepdims=True))
    main = main * inverse
    edge = edge * inverse
    main_w = main.astype(BF16)
    edge_w = edge.astype(BF16)
    main_g = nt(values, cots)
    edge_g = jnp.concatenate([nt(edge_values[i], cot_halves[i]) for i in range(2)], axis=1)
    delta = jnp.sum(main * main_g, axis=0, keepdims=True) + jnp.sum(edge * edge_g, axis=0, keepdims=True)
    main_s = (main * (main_g - delta) * SCALE).astype(BF16)
    edge_s = (edge * (edge_g - delta) * SCALE).astype(BF16)
    sides = [slice(0, BLK), slice(BLK, 2 * BLK)]
    out = tn(main_w, values) + jnp.concatenate(
        [tn(edge_w[:, sides[i]], edge_values[i]) for i in range(2)], axis=0
    )
    out_ref[...] = out.astype(BF16)
    dq_ref[...] = tn(main_s, keys) + jnp.concatenate(
        [tn(edge_s[:, sides[i]], edge_keys[i]) for i in range(2)], axis=0
    )
    dkeys = nn(main_s, queries)
    dvalues = nn(main_w, cots)
    dk_ref[...] = dkeys[:256]
    dv_ref[...] = dvalues[:256]
    drand_ref[0] = dkeys[256:384].astype(BF16)
    drand_ref[1] = dvalues[256:384].astype(BF16)
    part_ref[:, 0] = dkeys[384:].astype(BF16).reshape(NZ, 32, HEAD_DIM)
    part_ref[:, 1] = dvalues[384:].astype(BF16).reshape(NZ, 32, HEAD_DIM)
    for i in range(2):
        edge_ref[i, 0] = nn(edge_s[:, sides[i]], halves[i]).astype(BF16)
        edge_ref[i, 1] = nn(edge_w[:, sides[i]], cot_halves[i]).astype(BF16)


def grads_kernel(
    flip, k_ref, v_ref, gath_ref, stat_ref, drand_ref, edge_ref,
    dk_ref, dv_ref, part_ref, first_ref, last_ref, back_ref,
    edge_send, edge_recv, swap_send, swap_recv,
):
    me, x, z, y = place()
    tp = lax.axis_index("tp")
    heads = k_ref.shape[1] // HEAD_DIM
    after, before = line_peers(me, tp)
    partner = (seq_of(x, flipped(z, flip), y), tp)
    greet([after, before] + ([partner] if flip else []))
    returns = [
        remote(drand_ref.at[i], back_ref.at[i], swap_send.at[i], swap_recv.at[i], partner)
        for i in range(2 if flip else 0)
    ]
    for number in range(2):
        returns.append(
            remote(edge_ref.at[1, number], first_ref.at[number], edge_send.at[number], edge_recv.at[number], after)
        )
        returns.append(
            remote(edge_ref.at[0, number], last_ref.at[number], edge_send.at[2 + number], edge_recv.at[2 + number], before)
        )
    for copy in returns:
        copy.start()
    if flip == 0:
        back_ref[...] = drand_ref[...]

    def global_grads(head, carry):
        columns = head_columns(head)
        keys, values = k_ref[:, columns], v_ref[:, columns]
        queries = gath_ref[:, 0, :, columns].reshape(256, HEAD_DIM)
        cots = gath_ref[:, 3, :, columns].reshape(256, HEAD_DIM)
        row = pl.ds(head, 1)
        probs = jnp.exp(nt(keys, queries) * SCALE - stat_ref[0, row, :]) * stat_ref[1, row, :]
        slopes = nt(values, cots)
        scores = (probs * (slopes - stat_ref[2, row, :]) * SCALE).astype(BF16)
        weights = probs.astype(BF16)
        dk_ref[:, columns] = nn(scores, queries)
        dv_ref[:, columns] = nn(weights, cots)
        part_ref[:, 0, :, columns] = tn(scores, keys).astype(BF16).reshape(NZ, 32, HEAD_DIM)
        part_ref[:, 1, :, columns] = tn(weights, values).astype(BF16).reshape(NZ, 32, HEAD_DIM)
        return carry

    lax.fori_loop(0, heads, global_grads, 0)
    for copy in returns:
        copy.wait()


def reduce_kernel(
    flip, low_ref, high_ref, back_ref, total_ref, home_ref,
    out_ring, in_ring, out_piece, in_piece, ring_send, ring_recv, plane_send, plane_recv, swap_send, swap_recv,
):
    me, x, z, y = place()
    tp = lax.axis_index("tp")
    peers = plane_peers(x, z, y, tp)
    right, left = ring_peers(x, z, y, tp)
    mine = x * NY + y
    greet([peer for _, _, peer in peers] + [right, left])

    def part(target, number):
        return low_ref.at[target, number] if number < 2 else high_ref.at[target, number - 2]

    def hop(way, step, number):
        far = steps_of(number)[way] - step + 1
        target = lax.rem(z + far, NZ) if way == 0 else lax.rem(z + NZ - far, NZ)
        slot = (way * 4 + step - 1) * 4 + number
        if step == 1:
            source = part(target, number)
        else:
            source = out_ring.at[way, step - 1, number]
            source[...] = (
                part(target, number)[...].astype(F32) + in_ring[way, step - 2, number].astype(F32)
            ).astype(BF16)
        return remote(
            source, in_ring.at[way, step - 1, number], ring_send.at[slot], ring_recv.at[slot],
            right if way == 0 else left,
        )

    flying = {}
    for number in (2, 3, 0, 1):
        for way in range(2):
            flying[way, 1, number] = hop(way, 1, number)
            flying[way, 1, number].start()
    swaps = swap_in_plane(flip, x, z, y, tp, back_ref, home_ref, swap_send, swap_recv)
    if flip == 0:
        home_ref[...] = back_ref[...]
    sums = [None] * 4
    for step in range(1, 5):
        for number in (2, 3, 0, 1):
            for way in range(2):
                if step <= steps_of(number)[way]:
                    flying[way, step, number].wait_recv()
                    if step < steps_of(number)[way]:
                        flying[way, step + 1, number] = hop(way, step + 1, number)
                        flying[way, step + 1, number].start()
    for number in range(4):
        steps = steps_of(number)
        sums[number] = (
            part(z, number)[...].astype(F32)
            + in_ring[0, steps[0] - 1, number].astype(F32)
            + in_ring[1, steps[1] - 1, number].astype(F32)
        ).astype(BF16)
    stacked = jnp.concatenate(sums, axis=0)
    out_row = lax.broadcasted_iota(jnp.int32, (128, 128), 0)
    in_row = lax.broadcasted_iota(jnp.int32, (128, 128), 1)
    source_row = ((out_row % 16) // 4) * 32 + (out_row // 16) * 4 + out_row % 4
    order = jnp.where(in_row == source_row, 1.0, 0.0).astype(BF16)
    out_piece[...] = nn(order, stacked).astype(BF16).reshape(NP, 16, -1)
    copies = []
    for offset, number, peer in peers:
        copy = remote(
            out_piece.at[number], in_piece.at[offset], plane_send.at[offset], plane_recv.at[offset], peer
        )
        copy.start()
        copies.append(copy)
    total = out_piece[mine].astype(F32)
    for copy in copies:
        copy.wait()
    for offset in range(1, NP):
        total = total + in_piece[offset].astype(F32)
    total_ref[...] = total
    for copy in flying.values():
        copy.wait_send()
    for swap in swaps:
        swap.wait()


def finish_kernel(
    info_ref, out_ref, dq_ref, dk_ref, dv_ref, gdk_ref, gdv_ref, total_ref, first_ref, last_ref, rand_ref,
    attention_ref, gq_ref, gk_ref, gv_ref,
):
    rows = lax.broadcasted_iota(jnp.int32, (256, 16), 0)
    columns = lax.broadcasted_iota(jnp.int32, (256, 16), 1)
    hit = rows == position_of(info_ref, columns)
    total = total_ref[...]
    high = total.astype(BF16)
    low = (total - high.astype(F32)).astype(BF16)

    def rows_of(number, with_low):
        pick = jnp.where(hit & (columns // 4 == number), 1.0, 0.0).astype(BF16)
        placed = nn(pick, high)
        return placed + nn(pick, low) if with_low else placed

    gq_ref[...] = (dq_ref[...] + rows_of(0, True)).astype(BF16)
    attention_ref[...] = jnp.where(
        is_global(info_ref, out_ref.shape, 0), rows_of(1, False).astype(BF16), out_ref[...]
    )
    token = lax.broadcasted_iota(jnp.int32, out_ref.shape, 0)
    landing = token // BLK == info_ref[4]
    for number, (own_ref, all_ref, grad_ref) in enumerate(((dk_ref, gdk_ref, gk_ref), (dv_ref, gdv_ref, gv_ref))):
        back = rand_ref[number].astype(F32)
        edges = jnp.concatenate(
            [first_ref[number].astype(F32), last_ref[number].astype(F32)], axis=0
        )
        borrowed = jnp.where(landing, jnp.concatenate([back, back], axis=0), 0.0)
        grad_ref[...] = (own_ref[...] + all_ref[...] + edges + borrowed + rows_of(2 + number, True)).astype(BF16)


VMEM = pl.BlockSpec(memory_space=pltpu.VMEM)
DMA = pltpu.SemaphoreType.DMA


def params(collective_id=None):
    return pltpu.CompilerParams(
        collective_id=collective_id,
        has_side_effects=collective_id is not None,
        vmem_limit_bytes=56 * 1024 * 1024,
    )


def per_device(query_rows, key_rows, value_rows, cotangent, global_pos, partner_mask, rand_block):
    count, columns = query_rows.shape
    me = lax.axis_index("seq")
    mask = partner_mask[0]
    chosen = rand_block[0, jnp.bitwise_xor(me, mask)]
    number = jnp.arange(8, dtype=jnp.int32)
    info = jnp.where(number == 4, chosen, me.astype(jnp.int32))
    info = jnp.where(number < 4, jnp.pad(global_pos, (0, 4)) - me * count, info)

    def shape(*dims, dtype=BF16):
        return jax.ShapeDtypeStruct(dims, dtype)

    pair = shape(2, BLK, columns)
    wide_sum = shape(count, columns, dtype=F32)
    stats = shape(3, 8, 256, dtype=F32)
    half = shape(NZ, 2, 32, columns)
    in_smem = pl.BlockSpec(memory_space=pltpu.SMEM)

    in_plane = jnp.right_shift(mask, 5) * NY + jnp.bitwise_and(mask, 3)
    along_z = jnp.bitwise_and(jnp.right_shift(mask, 2), 7)

    def chosen_by(index, build, *operands):
        return lax.switch(index, [build(flip) for flip in range(8)], *operands)

    def gather(flip):
        return pl.pallas_call(
            functools.partial(gather_kernel, flip),
            out_shape=(shape(NZ, 4, 32, columns), pair),
            in_specs=[in_smem] + [VMEM] * 4,
            out_specs=(VMEM,) * 2,
            scratch_shapes=[
                pltpu.VMEM(pair.shape, BF16), pltpu.VMEM((NP, 16, columns), BF16),
                DMA((8,)), DMA((8,)), DMA((32,)), DMA((32,)), DMA((2,)), DMA((2,)),
            ],
            compiler_params=params(flip),
        )

    gath, passed = chosen_by(in_plane, gather, info, query_rows, key_rows, value_rows, cotangent)

    def prepare(flip):
        one, eight = pltpu.VMEM((3, 8, 256), F32), pltpu.VMEM((8, 3, 8, 256), F32)
        return pl.pallas_call(
            functools.partial(stats_kernel, flip),
            out_shape=(pair, pair, pair, stats),
            in_specs=[VMEM] * 4,
            out_specs=(VMEM,) * 4,
            scratch_shapes=[
                one, eight, one, eight,
                DMA((8,)), DMA((8,)), DMA((8,)), DMA((8,)), DMA((4,)), DMA((4,)), DMA((2,)), DMA((2,)),
            ],
            compiler_params=params(8 + flip),
        )

    prev, following, borrowed, stat = chosen_by(along_z, prepare, key_rows, value_rows, passed, gath)

    def by_columns(width, *lead):
        return pl.BlockSpec((*lead, width), lambda i: (*([0] * len(lead)), i))

    own = by_columns(HEAD_DIM, count)
    block = by_columns(HEAD_DIM, 2, BLK)
    out, dq, dk, dv, drand, edge, high = pl.pallas_call(
        attend_kernel,
        grid=(columns // HEAD_DIM,),
        out_shape=(
            shape(count, columns), wide_sum, wide_sum, wide_sum, pair, shape(2, 2, BLK, columns), half,
        ),
        in_specs=[in_smem] + [own] * 4 + [block] * 3 + [by_columns(HEAD_DIM, NZ, 4, 32)],
        out_specs=(own, own, own, own, block, by_columns(HEAD_DIM, 2, 2, BLK), by_columns(HEAD_DIM, NZ, 2, 32)),
        compiler_params=params(),
    )(info, query_rows, key_rows, value_rows, cotangent, prev, following, borrowed, gath)

    def grads(flip):
        return pl.pallas_call(
            functools.partial(grads_kernel, flip),
            out_shape=(wide_sum, wide_sum, half, pair, pair, pair),
            in_specs=[VMEM] * 6,
            out_specs=(VMEM,) * 6,
            scratch_shapes=[DMA((4,)), DMA((4,)), DMA((2,)), DMA((2,))],
            compiler_params=params(16 + flip),
        )

    gdk, gdv, low, first, last, back = chosen_by(along_z, grads, key_rows, value_rows, gath, stat, drand, edge)

    def reduce(flip):
        return pl.pallas_call(
            functools.partial(reduce_kernel, flip),
            out_shape=(shape(16, columns, dtype=F32), pair),
            in_specs=[VMEM] * 3,
            out_specs=(VMEM,) * 2,
            scratch_shapes=[
                pltpu.VMEM((2, 4, 4, 32, columns), BF16), pltpu.VMEM((2, 4, 4, 32, columns), BF16),
                pltpu.VMEM((NP, 16, columns), BF16), pltpu.VMEM((NP, 16, columns), BF16),
                DMA((32,)), DMA((32,)), DMA((8,)), DMA((8,)), DMA((2,)), DMA((2,)),
            ],
            compiler_params=params(24 + flip),
        )

    total, returned = chosen_by(in_plane, reduce, low, high, back)

    own = by_columns(256, count)
    block = by_columns(256, 2, BLK)
    return pl.pallas_call(
        finish_kernel,
        grid=(columns // 256,),
        out_shape=(shape(count, columns),) * 4,
        in_specs=[in_smem] + [own] * 6 + [by_columns(256, 16)] + [block] * 3,
        out_specs=(own,) * 4,
        compiler_params=params(),
    )(info, out, dq, dk, dv, gdk, gdv, total, first, last, returned)


def solution(mesh):
    placed = (P("seq", "tp"),) * 4 + (P("seq"), P(), P())
    return jax.shard_map(
        per_device,
        mesh=mesh,
        in_specs=placed,
        out_specs=(P("seq", "tp"),) * 4,
        check_vma=False,
    )
```

```python
import functools

import jax
import jax.numpy as jnp
from jax import lax
from jax.experimental import pallas as pl
from jax.experimental.pallas import tpu as pltpu
from jax.sharding import PartitionSpec as P

HEAD_DIM = 128
BLK = 128
NX, NZ, NY = 2, 8, 4
NP = NX * NY
SCALE = HEAD_DIM**-0.5
MESH = pl.DeviceIdType.MESH
F32 = jnp.float32
BF16 = jnp.bfloat16


def nt(a, b):
    return lax.dot_general(a, b, (((1,), (1,)), ((), ())), preferred_element_type=F32)


def nn(a, b):
    return lax.dot_general(a, b, (((1,), (0,)), ((), ())), preferred_element_type=F32)


def tn(a, b):
    return lax.dot_general(a, b, (((0,), (0,)), ((), ())), preferred_element_type=F32)


def place():
    me = lax.axis_index("seq")
    return me, me // (NZ * NY), (me // NY) % NZ, me % NY


def seq_of(x, z, y):
    return (x * NZ + z) * NY + y


def greet(peers):
    barrier = pltpu.get_barrier_semaphore()
    for peer in peers:
        pl.semaphore_signal(barrier, inc=1, device_id=peer, device_id_type=MESH)
    pl.semaphore_wait(barrier, len(peers))


def plane_peers(x, z, y, tp):
    peers = []
    for offset in range(1, NP):
        dx, dy = offset // NY, offset % NY
        px, py = lax.rem(x + dx, NX), lax.rem(y + dy, NY)
        peers.append((offset, px * NY + py, (seq_of(px, z, py), tp)))
    return peers


def ring_peers(x, z, y, tp):
    return (seq_of(x, lax.rem(z + 1, NZ), y), tp), (seq_of(x, lax.rem(z + NZ - 1, NZ), y), tp)


def flipped(value, flip):
    bit = 1
    while bit <= flip:
        if flip & bit:
            value = value + bit * (1 - 2 * ((value // bit) % 2))
        bit *= 2
    return value


def line_peers(me, tp):
    return (lax.rem(me + 1, NX * NZ * NY), tp), (lax.rem(me + NX * NZ * NY - 1, NX * NZ * NY), tp)


def remote(src, dst, send, recv, device):
    return pltpu.make_async_remote_copy(
        src_ref=src, dst_ref=dst, send_sem=send, recv_sem=recv, device_id=device, device_id_type=MESH
    )


def position_of(info_ref, rows):
    turn = rows % 4
    found = jnp.where(turn == 0, info_ref[0], info_ref[1])
    return jnp.where(turn == 2, info_ref[2], jnp.where(turn == 3, info_ref[3], found))


def is_global(info_ref, shape, dimension):
    token = lax.broadcasted_iota(jnp.int32, shape, dimension)
    hit = token == info_ref[0]
    for number in range(1, 4):
        hit = hit | (token == info_ref[number])
    return hit


def head_columns(head):
    return pl.ds(pl.multiple_of(head * HEAD_DIM, HEAD_DIM), HEAD_DIM)


def swap_along_z(flip, x, z, y, tp, source, target, send, recv, others):
    device = (seq_of(x, flipped(z, flip), y), tp)
    greet(others + ([device] if flip else []))
    if flip == 0:
        return []
    swaps = [
        remote(source.at[number], target.at[number], send.at[number], recv.at[number], device)
        for number in range(2)
    ]
    for swap in swaps:
        swap.start()
    return swaps


def swap_in_plane(flip, x, z, y, tp, source, target, send, recv):
    if flip == 0:
        return []
    device = (seq_of(flipped(x, flip // NY), z, flipped(y, flip % NY)), tp)
    swaps = [
        remote(source.at[number], target.at[number], send.at[number], recv.at[number], device)
        for number in range(2)
    ]
    for swap in swaps:
        swap.start()
    return swaps


def steps_of(array):
    return (4, 3) if array < 2 else (3, 4)


def gather_kernel(
    flip, info_ref, q_ref, k_ref, v_ref, c_ref, gath_ref, passed_ref,
    parcel_ref, piece_ref, plane_send, plane_recv, ring_send, ring_recv, swap_send, swap_recv,
):
    me, x, z, y = place()
    tp = lax.axis_index("tp")
    peers = plane_peers(x, z, y, tp)
    right, left = ring_peers(x, z, y, tp)
    mine = x * NY + y

    rows = lax.broadcasted_iota(jnp.int32, (16, 256), 0)
    columns = lax.broadcasted_iota(jnp.int32, (16, 256), 1)
    hit = columns == position_of(info_ref, rows)
    total = jnp.zeros((16, q_ref.shape[1]), F32)
    for number, ref in enumerate((q_ref, k_ref, v_ref, c_ref)):
        pick = jnp.where(hit & (rows // 4 == number), 1.0, 0.0).astype(BF16)
        total = total + nn(pick, ref[...])
    piece_ref[mine] = total.astype(BF16)
    target = parcel_ref if flip else passed_ref
    for number, ref in enumerate((k_ref, v_ref)):
        target[number] = jnp.where(info_ref[4] == 1, ref[BLK:], ref[:BLK])

    greet([peer for _, _, peer in peers] + [right, left])
    copies = []
    for offset, _, peer in peers:
        copy = remote(
            piece_ref.at[mine], piece_ref.at[mine], plane_send.at[offset], plane_recv.at[offset], peer
        )
        copy.start()
        copies.append(copy)
    swaps = swap_in_plane(flip, x, z, y, tp, parcel_ref, passed_ref, swap_send, swap_recv)
    for copy in copies:
        copy.wait()

    out_row = lax.broadcasted_iota(jnp.int32, (32, 128), 0)
    in_row = lax.broadcasted_iota(jnp.int32, (32, 128), 1)
    pieces = piece_ref[...].reshape(128, -1)
    for number in range(4):
        pick = jnp.where(in_row == (out_row // 4) * 16 + number * 4 + out_row % 4, 1.0, 0.0)
        gath_ref[z, number] = nn(pick.astype(BF16), pieces).astype(BF16)

    def hop(way, step, number):
        shift = lax.rem(z + NZ - step + 1, NZ) if way == 0 else lax.rem(z + step - 1, NZ)
        slot = (way * 4 + step - 1) * 4 + number
        part = gath_ref.at[shift, number]
        return remote(part, part, ring_send.at[slot], ring_recv.at[slot], right if way == 0 else left)

    flying = {}
    for number in range(4):
        for way in range(2):
            flying[way, 1, number] = hop(way, 1, number)
            flying[way, 1, number].start()
    for step in range(1, 5):
        for number in range(4):
            for way in range(2):
                if step <= steps_of(number)[way]:
                    flying[way, step, number].wait_recv()
                    if step < steps_of(number)[way]:
                        flying[way, step + 1, number] = hop(way, step + 1, number)
                        flying[way, step + 1, number].start()
    for copy in flying.values():
        copy.wait_send()
    for swap in swaps:
        swap.wait()


def join(ref):
    top = ref[0, 0]
    for number in range(1, 8):
        top = jnp.maximum(top, ref[number, 0])
    total = jnp.zeros_like(top)
    slope = jnp.zeros_like(top)
    for number in range(8):
        factor = jnp.exp(ref[number, 0] - top)
        total = total + ref[number, 1] * factor
        slope = slope + ref[number, 2] * factor
    return top, total, slope


def stats_kernel(
    flip, k_ref, v_ref, passed_ref, gath_ref, rand_ref, prev_ref, next_ref, stat_ref,
    swap_send, swap_recv, edge_send, edge_recv,
):
    me, x, z, y = place()
    tp = lax.axis_index("tp")
    heads = k_ref.shape[1] // HEAD_DIM
    after, before = line_peers(me, tp)
    swaps = swap_along_z(flip, x, z, y, tp, passed_ref, rand_ref, swap_send, swap_recv, [after, before])
    width = prev_ref.shape[2]
    edges = []
    for i, ref in enumerate((k_ref, v_ref)):
        for way, target, rows, device in ((0, prev_ref, BLK, after), (1, next_ref, 0, before)):
            slot = i * 2 + way
            edges.append(
                remote(
                    ref.at[pl.ds(rows, BLK), pl.ds(0, width)], target.at[i],
                    edge_send.at[slot], edge_recv.at[slot], device,
                )
            )
    for edge in edges:
        edge.start()
    swaps = swaps + edges
    if flip == 0:
        rand_ref[...] = passed_ref[...]

    def global_stats(head, carry):
        columns = head_columns(head)
        queries = gath_ref[:, 0, :, columns].reshape(256, HEAD_DIM)
        cots = gath_ref[:, 3, :, columns].reshape(256, HEAD_DIM)
        scores = nt(k_ref[:, columns], queries) * SCALE
        slopes = nt(v_ref[:, columns], cots)
        top = jnp.max(scores, axis=0, keepdims=True)
        raised = jnp.exp(scores - top)
        stat_ref[0, pl.ds(head, 1), :] = top
        stat_ref[1, pl.ds(head, 1), :] = jnp.sum(raised, axis=0, keepdims=True)
        stat_ref[2, pl.ds(head, 1), :] = jnp.sum(raised * slopes, axis=0, keepdims=True)
        return carry

    lax.fori_loop(0, heads, global_stats, 0)
    for swap in swaps:
        swap.wait()


def attend_kernel(
    info_ref, q_ref, k_ref, v_ref, c_ref, rand_ref, gath_ref, all_k_ref, all_v_ref, had_prev_ref, had_next_ref,
    stat_ref, out_ref, dq_ref, dk_ref, dv_ref, drand_ref, part_ref, first_ref, last_ref, late_ref, final_ref,
    prev_ref, next_ref, edge_ref, home_first_ref, home_last_ref, ring_ref, mid_ref, plane_ref,
    ring_send, ring_recv, plane_send, plane_recv, edge_send, edge_recv, back_send, back_recv,
):
    me, x, z, y = place()
    tp = lax.axis_index("tp")
    peers = [(offset, peer) for offset, _, peer in plane_peers(x, z, y, tp)]
    rings = [(offset, (seq_of(x, lax.rem(z + offset, NZ), y), tp)) for offset in range(1, NZ)]
    after, before = line_peers(me, tp)
    head = pl.program_id(0)
    heads = all_k_ref.shape[1] // HEAD_DIM
    half = heads // 2
    ends = [peer for _, peer in rings + peers] + [after, before]

    def edges_in(number):
        columns, copies = head_columns(number), []
        for i, ref in enumerate((all_k_ref, all_v_ref)):
            for way, target, rows, device in ((0, prev_ref, BLK, after), (1, next_ref, 0, before)):
                slot = (number * 2 + i) * 2 + way
                copies.append(
                    remote(
                        ref.at[pl.ds(rows, BLK), columns], target.at[i, :, columns],
                        edge_send.at[slot], edge_recv.at[slot], device,
                    )
                )
        return copies

    def edges_back(number):
        columns, copies = head_columns(number), []
        for i in range(2):
            for way, target, device in ((1, home_first_ref, after), (0, home_last_ref, before)):
                slot = (number * 2 + i) * 2 + way
                copies.append(
                    remote(
                        edge_ref.at[way, i, :, columns], target.at[i, :, columns],
                        back_send.at[slot], back_recv.at[slot], device,
                    )
                )
        return copies

    def along_ring():
        return [remote(ring_ref.at[0], ring_ref.at[i], ring_send.at[i], ring_recv.at[i], peer) for i, peer in rings]

    def in_plane():
        return [remote(mid_ref, plane_ref.at[i], plane_send.at[i], plane_recv.at[i], peer) for i, peer in peers]

    @pl.when(head == 0)
    def _():
        ring_ref[0] = stat_ref[...]
        greet(ends)
        for copy in along_ring():
            copy.start()
        for number in range(half, heads):
            for copy in edges_in(number):
                copy.start()
        width = had_prev_ref.shape[2]
        prev_ref[:, :, :width] = had_prev_ref[...]
        next_ref[:, :, :width] = had_next_ref[...]

    @pl.when(head == 5)
    def _():
        for copy in along_ring():
            copy.wait()
        for number, value in enumerate(join(ring_ref)):
            mid_ref[number] = value
        for copy in in_plane():
            copy.start()
        plane_ref[0] = mid_ref[...]

    @pl.when((head > 0) & (head <= half))
    def _():
        for copy in edges_back(head - 1):
            copy.start()

    @pl.when(head >= half)
    def _():
        for copy in edges_in(head):
            copy.wait()

    columns = head_columns(head)
    queries = q_ref[...]
    hit = is_global(info_ref, (256, HEAD_DIM), 0)
    cots = jnp.where(hit, jnp.zeros((256, HEAD_DIM), BF16), c_ref[...])
    keys = jnp.concatenate([k_ref[...], rand_ref[0], gath_ref[:, 1].reshape(256, HEAD_DIM)], axis=0)
    values = jnp.concatenate([v_ref[...], rand_ref[1], gath_ref[:, 2].reshape(256, HEAD_DIM)], axis=0)
    edge_keys = (prev_ref[0, :, columns], next_ref[0, :, columns])
    edge_values = (prev_ref[1, :, columns], next_ref[1, :, columns])
    halves = (queries[:BLK], queries[BLK:])
    cot_halves = (cots[:BLK], cots[BLK:])
    token = lax.broadcasted_iota(jnp.int32, (1, 2 * BLK), 1)
    closed = ((token < BLK) & (info_ref[5] == 0)) | ((token >= BLK) & (info_ref[5] == NX * NZ * NY - 1))
    bias = jnp.where(closed, -1e30, 0.0)
    main = nt(keys, queries) * SCALE
    edge = jnp.concatenate([nt(edge_keys[i], halves[i]) for i in range(2)], axis=1) * SCALE + bias
    top = jnp.maximum(jnp.max(main, axis=0, keepdims=True), jnp.max(edge, axis=0, keepdims=True))
    main = jnp.exp(main - top)
    edge = jnp.exp(edge - top)
    inverse = 1.0 / (jnp.sum(main, axis=0, keepdims=True) + jnp.sum(edge, axis=0, keepdims=True))
    main = main * inverse
    edge = edge * inverse
    main_w = main.astype(BF16)
    edge_w = edge.astype(BF16)
    main_g = nt(values, cots)
    edge_g = jnp.concatenate([nt(edge_values[i], cot_halves[i]) for i in range(2)], axis=1)
    delta = jnp.sum(main * main_g, axis=0, keepdims=True) + jnp.sum(edge * edge_g, axis=0, keepdims=True)
    main_s = (main * (main_g - delta) * SCALE).astype(BF16)
    edge_s = (edge * (edge_g - delta) * SCALE).astype(BF16)
    sides = [slice(0, BLK), slice(BLK, 2 * BLK)]
    out = tn(main_w, values) + jnp.concatenate(
        [tn(edge_w[:, sides[i]], edge_values[i]) for i in range(2)], axis=0
    )
    out_ref[...] = out.astype(BF16)
    dq_ref[...] = tn(main_s, keys) + jnp.concatenate(
        [tn(edge_s[:, sides[i]], edge_keys[i]) for i in range(2)], axis=0
    )
    dkeys = nn(main_s, queries)
    dvalues = nn(main_w, cots)
    dk_ref[...] = dkeys[:256]
    dv_ref[...] = dvalues[:256]
    drand_ref[0] = dkeys[256:384].astype(BF16)
    drand_ref[1] = dvalues[256:384].astype(BF16)
    part_ref[:, 0] = dkeys[384:].astype(BF16).reshape(NZ, 32, HEAD_DIM)
    part_ref[:, 1] = dvalues[384:].astype(BF16).reshape(NZ, 32, HEAD_DIM)
    for i in range(2):
        edge_ref[i, 0, :, columns] = nn(edge_s[:, sides[i]], halves[i]).astype(BF16)
        edge_ref[i, 1, :, columns] = nn(edge_w[:, sides[i]], cot_halves[i]).astype(BF16)

    @pl.when(head == heads - 1)
    def _():
        for copy in in_plane():
            copy.wait()
        top, total, slope = join(plane_ref)
        inverse = 1.0 / total
        final_ref[0] = top
        final_ref[1] = inverse
        final_ref[2] = slope * inverse
        late_ref[...] = edge_ref[:, :, :, half * HEAD_DIM :]
        for number in range(half):
            for copy in edges_back(number):
                copy.wait()
        first_ref[...] = home_first_ref[...]
        last_ref[...] = home_last_ref[...]


def grads_kernel(
    flip, k_ref, v_ref, gath_ref, stat_ref, drand_ref, late_ref,
    dk_ref, dv_ref, part_ref, back_ref, first_ref, last_ref,
    swap_send, swap_recv, edge_send, edge_recv,
):
    me, x, z, y = place()
    tp = lax.axis_index("tp")
    heads = k_ref.shape[1] // HEAD_DIM
    after, before = line_peers(me, tp)
    returns = swap_along_z(flip, x, z, y, tp, drand_ref, back_ref, swap_send, swap_recv, [after, before])
    edges = []
    for i in range(2):
        for way, target, device in ((1, first_ref, after), (0, last_ref, before)):
            slot = i * 2 + way
            edges.append(
                remote(late_ref.at[way, i], target.at[i], edge_send.at[slot], edge_recv.at[slot], device)
            )
    for edge in edges:
        edge.start()
    returns = returns + edges
    if flip == 0:
        back_ref[...] = drand_ref[...]

    def global_grads(head, carry):
        columns = head_columns(head)
        keys, values = k_ref[:, columns], v_ref[:, columns]
        queries = gath_ref[:, 0, :, columns].reshape(256, HEAD_DIM)
        cots = gath_ref[:, 3, :, columns].reshape(256, HEAD_DIM)
        row = pl.ds(head, 1)
        probs = jnp.exp(nt(keys, queries) * SCALE - stat_ref[0, row, :]) * stat_ref[1, row, :]
        slopes = nt(values, cots)
        scores = (probs * (slopes - stat_ref[2, row, :]) * SCALE).astype(BF16)
        weights = probs.astype(BF16)
        dk_ref[:, columns] = nn(scores, queries)
        dv_ref[:, columns] = nn(weights, cots)
        part_ref[:, 0, :, columns] = tn(scores, keys).astype(BF16).reshape(NZ, 32, HEAD_DIM)
        part_ref[:, 1, :, columns] = tn(weights, values).astype(BF16).reshape(NZ, 32, HEAD_DIM)
        return carry

    lax.fori_loop(0, heads, global_grads, 0)
    for copy in returns:
        copy.wait()


def reduce_kernel(
    flip, low_ref, high_ref, back_ref, total_ref, home_ref,
    out_ring, in_ring, out_piece, in_piece, ring_send, ring_recv, plane_send, plane_recv, swap_send, swap_recv,
):
    me, x, z, y = place()
    tp = lax.axis_index("tp")
    peers = plane_peers(x, z, y, tp)
    right, left = ring_peers(x, z, y, tp)
    mine = x * NY + y
    greet([peer for _, _, peer in peers] + [right, left])

    def part(target, number):
        return low_ref.at[target, number] if number < 2 else high_ref.at[target, number - 2]

    def hop(way, step, number):
        far = steps_of(number)[way] - step + 1
        target = lax.rem(z + far, NZ) if way == 0 else lax.rem(z + NZ - far, NZ)
        slot = (way * 4 + step - 1) * 4 + number
        if step == 1:
            source = part(target, number)
        else:
            source = out_ring.at[way, step - 1, number]
            source[...] = (
                part(target, number)[...].astype(F32) + in_ring[way, step - 2, number].astype(F32)
            ).astype(BF16)
        return remote(
            source, in_ring.at[way, step - 1, number], ring_send.at[slot], ring_recv.at[slot],
            right if way == 0 else left,
        )

    flying = {}
    for number in (2, 3, 0, 1):
        for way in range(2):
            flying[way, 1, number] = hop(way, 1, number)
            flying[way, 1, number].start()
    swaps = swap_in_plane(flip, x, z, y, tp, back_ref, home_ref, swap_send, swap_recv)
    if flip == 0:
        home_ref[...] = back_ref[...]
    sums = [None] * 4
    for step in range(1, 5):
        for number in (2, 3, 0, 1):
            for way in range(2):
                if step <= steps_of(number)[way]:
                    flying[way, step, number].wait_recv()
                    if step < steps_of(number)[way]:
                        flying[way, step + 1, number] = hop(way, step + 1, number)
                        flying[way, step + 1, number].start()
    for number in range(4):
        steps = steps_of(number)
        sums[number] = (
            part(z, number)[...].astype(F32)
            + in_ring[0, steps[0] - 1, number].astype(F32)
            + in_ring[1, steps[1] - 1, number].astype(F32)
        ).astype(BF16)
    stacked = jnp.concatenate(sums, axis=0)
    out_row = lax.broadcasted_iota(jnp.int32, (128, 128), 0)
    in_row = lax.broadcasted_iota(jnp.int32, (128, 128), 1)
    source_row = ((out_row % 16) // 4) * 32 + (out_row // 16) * 4 + out_row % 4
    order = jnp.where(in_row == source_row, 1.0, 0.0).astype(BF16)
    out_piece[...] = nn(order, stacked).astype(BF16).reshape(NP, 16, -1)
    copies = []
    for offset, number, peer in peers:
        copy = remote(
            out_piece.at[number], in_piece.at[offset], plane_send.at[offset], plane_recv.at[offset], peer
        )
        copy.start()
        copies.append(copy)
    total = out_piece[mine].astype(F32)
    for copy in copies:
        copy.wait()
    for offset in range(1, NP):
        total = total + in_piece[offset].astype(F32)
    total_ref[...] = total
    for copy in flying.values():
        copy.wait_send()
    for swap in swaps:
        swap.wait()


def finish_kernel(
    info_ref, out_ref, dq_ref, dk_ref, dv_ref, gdk_ref, gdv_ref, total_ref,
    first_ref, last_ref, late_first_ref, late_last_ref, rand_ref,
    attention_ref, gq_ref, gk_ref, gv_ref,
):
    rows = lax.broadcasted_iota(jnp.int32, (256, 16), 0)
    columns = lax.broadcasted_iota(jnp.int32, (256, 16), 1)
    hit = rows == position_of(info_ref, columns)
    total = total_ref[...]
    high = total.astype(BF16)
    low = (total - high.astype(F32)).astype(BF16)

    def rows_of(number, with_low):
        pick = jnp.where(hit & (columns // 4 == number), 1.0, 0.0).astype(BF16)
        placed = nn(pick, high)
        return placed + nn(pick, low) if with_low else placed

    gq_ref[...] = (dq_ref[...] + rows_of(0, True)).astype(BF16)
    attention_ref[...] = jnp.where(
        is_global(info_ref, out_ref.shape, 0), rows_of(1, False).astype(BF16), out_ref[...]
    )
    token = lax.broadcasted_iota(jnp.int32, out_ref.shape, 0)
    landing = token // BLK == info_ref[4]
    for number, (own_ref, all_ref, grad_ref) in enumerate(((dk_ref, gdk_ref, gk_ref), (dv_ref, gdv_ref, gv_ref))):
        back = rand_ref[number].astype(F32)
        early = jnp.concatenate([first_ref[number], last_ref[number]], axis=0).astype(F32)
        late = jnp.concatenate([late_first_ref[number], late_last_ref[number]], axis=0).astype(F32)
        edges = jnp.where(pl.program_id(0) < pl.num_programs(0) // 2, early, late)
        borrowed = jnp.where(landing, jnp.concatenate([back, back], axis=0), 0.0)
        grad_ref[...] = (own_ref[...] + all_ref[...] + edges + borrowed + rows_of(2 + number, True)).astype(BF16)


VMEM = pl.BlockSpec(memory_space=pltpu.VMEM)
DMA = pltpu.SemaphoreType.DMA


def params(collective_id=None):
    return pltpu.CompilerParams(
        collective_id=collective_id,
        has_side_effects=collective_id is not None,
        vmem_limit_bytes=56 * 1024 * 1024,
    )


def per_device(query_rows, key_rows, value_rows, cotangent, global_pos, partner_mask, rand_block):
    count, columns = query_rows.shape
    me = lax.axis_index("seq")
    mask = partner_mask[0]
    chosen = rand_block[0, jnp.bitwise_xor(me, mask)]
    number = jnp.arange(8, dtype=jnp.int32)
    info = jnp.where(number == 4, chosen, me.astype(jnp.int32))
    info = jnp.where(number < 4, jnp.pad(global_pos, (0, 4)) - me * count, info)

    def shape(*dims, dtype=BF16):
        return jax.ShapeDtypeStruct(dims, dtype)

    pair = shape(2, BLK, columns)
    half_pair = shape(2, BLK, columns // 2)
    wide_sum = shape(count, columns, dtype=F32)
    stats = shape(3, 8, 256, dtype=F32)
    half = shape(NZ, 2, 32, columns)
    in_smem = pl.BlockSpec(memory_space=pltpu.SMEM)

    in_plane = jnp.right_shift(mask, 5) * NY + jnp.bitwise_and(mask, 3)
    along_z = jnp.bitwise_and(jnp.right_shift(mask, 2), 7)

    def chosen_by(index, build, *operands):
        return lax.switch(index, [build(flip) for flip in range(8)], *operands)

    def gather(flip):
        return pl.pallas_call(
            functools.partial(gather_kernel, flip),
            out_shape=(shape(NZ, 4, 32, columns), pair),
            in_specs=[in_smem] + [VMEM] * 4,
            out_specs=(VMEM,) * 2,
            scratch_shapes=[
                pltpu.VMEM(pair.shape, BF16), pltpu.VMEM((NP, 16, columns), BF16),
                DMA((8,)), DMA((8,)), DMA((32,)), DMA((32,)), DMA((2,)), DMA((2,)),
            ],
            compiler_params=params(flip),
        )

    gath, passed = chosen_by(in_plane, gather, info, query_rows, key_rows, value_rows, cotangent)

    def prepare(flip):
        return pl.pallas_call(
            functools.partial(stats_kernel, flip),
            out_shape=(pair, half_pair, half_pair, stats),
            in_specs=[VMEM] * 4,
            out_specs=(VMEM,) * 4,
            scratch_shapes=[DMA((2,)), DMA((2,)), DMA((4,)), DMA((4,))],
            compiler_params=params(8 + flip),
        )

    borrowed, prev, following, stat = chosen_by(along_z, prepare, key_rows, value_rows, passed, gath)

    def by_columns(width, *lead):
        return pl.BlockSpec((*lead, width), lambda i: (*([0] * len(lead)), i))

    own = by_columns(HEAD_DIM, count)
    block = by_columns(HEAD_DIM, 2, BLK)
    edges = pltpu.VMEM(pair.shape, BF16)
    whole = pl.BlockSpec(memory_space=pl.ANY)
    one, eight = pltpu.VMEM((3, 8, 256), F32), pltpu.VMEM((8, 3, 8, 256), F32)
    out, dq, dk, dv, drand, high, first, last, late, final = pl.pallas_call(
        attend_kernel,
        grid=(columns // HEAD_DIM,),
        out_shape=(
            shape(count, columns), wide_sum, wide_sum, wide_sum, pair, half, half_pair, half_pair,
            shape(2, 2, BLK, columns // 2), stats,
        ),
        in_specs=[in_smem] + [own] * 4 + [block, by_columns(HEAD_DIM, NZ, 4, 32)] + [whole] * 2 + [VMEM] * 3,
        out_specs=(own, own, own, own, block, by_columns(HEAD_DIM, NZ, 2, 32)) + (VMEM,) * 4,
        scratch_shapes=[
            edges, edges, pltpu.VMEM((2, 2, BLK, columns), BF16), pltpu.VMEM(half_pair.shape, BF16),
            pltpu.VMEM(half_pair.shape, BF16), eight, one, eight,
            DMA((8,)), DMA((8,)), DMA((8,)), DMA((8,)), DMA((32,)), DMA((32,)), DMA((32,)), DMA((32,)),
        ],
        compiler_params=params(32),
    )(info, query_rows, key_rows, value_rows, cotangent, borrowed, gath, key_rows, value_rows, prev, following, stat)

    def grads(flip):
        return pl.pallas_call(
            functools.partial(grads_kernel, flip),
            out_shape=(wide_sum, wide_sum, half, pair, half_pair, half_pair),
            in_specs=[VMEM] * 6,
            out_specs=(VMEM,) * 6,
            scratch_shapes=[DMA((2,)), DMA((2,)), DMA((4,)), DMA((4,))],
            compiler_params=params(16 + flip),
        )

    gdk, gdv, low, back, late_first, late_last = chosen_by(
        along_z, grads, key_rows, value_rows, gath, final, drand, late
    )

    def reduce(flip):
        return pl.pallas_call(
            functools.partial(reduce_kernel, flip),
            out_shape=(shape(16, columns, dtype=F32), pair),
            in_specs=[VMEM] * 3,
            out_specs=(VMEM,) * 2,
            scratch_shapes=[
                pltpu.VMEM((2, 4, 4, 32, columns), BF16), pltpu.VMEM((2, 4, 4, 32, columns), BF16),
                pltpu.VMEM((NP, 16, columns), BF16), pltpu.VMEM((NP, 16, columns), BF16),
                DMA((32,)), DMA((32,)), DMA((8,)), DMA((8,)), DMA((2,)), DMA((2,)),
            ],
            compiler_params=params(24 + flip),
        )

    total, returned = chosen_by(in_plane, reduce, low, high, back)

    own = by_columns(256, count)
    block = by_columns(256, 2, BLK)
    turn = columns // 512
    early = pl.BlockSpec((2, BLK, 256), lambda i: (0, 0, jnp.minimum(i, turn - 1)))
    late_half = pl.BlockSpec((2, BLK, 256), lambda i: (0, 0, jnp.maximum(i - turn, 0)))
    return pl.pallas_call(
        finish_kernel,
        grid=(columns // 256,),
        out_shape=(shape(count, columns),) * 4,
        in_specs=[in_smem] + [own] * 6 + [by_columns(256, 16)] + [early] * 2 + [late_half] * 2 + [block],
        out_specs=(own,) * 4,
        compiler_params=params(),
    )(info, out, dq, dk, dv, gdk, gdv, total, first, last, late_first, late_last, returned)


def solution(mesh):
    placed = (P("seq", "tp"),) * 4 + (P("seq"), P(), P())
    return jax.shard_map(
        per_device,
        mesh=mesh,
        in_specs=placed,
        out_specs=(P("seq", "tp"),) * 4,
        check_vma=False,
    )
```
